32 devices in a mesh: bead: 4 (over x, core), slab: 8 (over z, y).
Axes of the slice: x: 2, y: 2, z: 4, core: 2. Of those that a mesh axis runs over, the one named last changes fastest.
Arguments:
- positions: float32 [16, 3, 8192], P('bead', None, 'slab'), may hold values from -0.4 to 16.4, as said below
- velocities: float32 [16, 3, 8192], P('bead', None, 'slab'), may hold values from -5 to 5
- masses: float32 [8192], P('slab'), may hold values from 1 to 16
- amplitudes: float32 [8192], P('slab'), may hold values from 0.15 to 0.6
- charges: float32 [8192], P('slab'), may hold values from -1.2 to 1.2
Outputs:
- moved: float32 [16, 3, 8192], P('bead', None, 'slab')
- final_velocities: float32 [16, 3, 8192], P('bead', None, 'slab')
The draws below stay inside these ranges and needn't reach their ends.
Inputs may be any that keep to these rules, and one draw needn't show every extreme that they name: `positions`: atom n's beads lie within 0.4 of its cell: plane n // 512 spans first coordinates from its index to its index plus one, and cell (n % 512) // 128 = 2 a + e of that plane spans second coordinates a to a + 1 and third coordinates e to e + 1.
All inputs are finite; a program needn't handle non-finite values.
Results may differ from the reference program's by a relative error of at most 0.0003.
Values sent between devices are 32-bit elements; how exact they have to be, the bound alone decides.
A program may use at most 64 MiB of HBM per device.

```python
import math
import jax
import jax.numpy as jnp
from jax import lax

CELL_ATOMS = 128
INNER_STEPS = 2
OUTER_STEPS = 2
PLANE_ATOMS = 512
BEADS = 16
CBEADS = 4
ATOMS = 8192


def draw_positions(key, part):
    first_key = jax.random.fold_in(key, 11)
    second_key = jax.random.fold_in(key, 23)
    third_key = jax.random.fold_in(key, 37)
    fourth_key = jax.random.fold_in(key, 41)
    index = jnp.arange(ATOMS, dtype=jnp.int32)
    plane = (index // PLANE_ATOMS).astype(jnp.float32)
    cell = index % PLANE_ATOMS // CELL_ATOMS
    corner = jnp.stack([plane, (cell // 2).astype(jnp.float32), (cell % 2).astype(jnp.float32)])
    centre = corner + jax.random.uniform(first_key, (3, ATOMS), jnp.float32)
    mode_count = CBEADS // 2 - 1
    modes = jnp.arange(1, mode_count + 1, dtype=jnp.float32)
    cycle_place = 2.0 * jnp.pi * jnp.arange(BEADS, dtype=jnp.float32) / BEADS
    angle = modes[:, None] * cycle_place[None, :]
    cosine = jnp.cos(angle)
    sine = jnp.sin(angle)
    factor = 0.15
    cos_coef = factor * jax.random.normal(second_key, (mode_count, 3, ATOMS), jnp.float32)
    sin_coef = factor * jax.random.normal(third_key, (mode_count, 3, ATOMS), jnp.float32)
    rough = jax.random.uniform(fourth_key, (BEADS, 3, ATOMS), jnp.float32, -0.08, 0.08)
    smooth = jnp.einsum('kb,kca->bca', cosine, cos_coef, precision=lax.Precision.HIGHEST)
    smooth = smooth + jnp.einsum('kb,kca->bca', sine, sin_coef, precision=lax.Precision.HIGHEST)
    spread = 0.3 * jnp.tanh(smooth / 0.3) + rough
    return centre[None] + spread


def level_of(own_key, shape, pieces, low, largest):
    def one(position, blocks):
        draws = jax.random.uniform(jax.random.fold_in(jax.random.fold_in(own_key, 6), position), (blocks,), jnp.float32, low / len(pieces), largest / len(pieces))
        return jnp.repeat(jnp.exp(draws), shape[position] // blocks).reshape((-1,) + (1,) * (len(shape) - position - 1))

    loudness = one(*pieces[0])
    for cut in pieces[1:]:
        loudness = loudness * one(*cut)
    return loudness


def gaussian(own_key, shape, scale, most, shards=(), kind=jnp.bfloat16):
    array = scale * jax.random.normal(own_key, shape, jnp.float32)
    if shards:
        array = array * level_of(own_key, shape, shards, -0.22, 0.18)
    return jnp.clip(array, -most, most).astype(kind)


def setup_inputs(seed: int = 0) -> dict:
    splits = jax.random.split(jax.random.key(seed), 6)
    positions = draw_positions(jax.random.fold_in(splits[5], 71), 0)
    velocities = gaussian(splits[1], (BEADS, 3, ATOMS), 1.0, 5.0, ((0, 4), (2, 8)), jnp.float32)
    masses = jnp.clip(jnp.exp(math.log(16.0) - 2.7725887 * jax.random.uniform(splits[2], (ATOMS,), jnp.float32) ** level_of(splits[2], (ATOMS,), ((0, 8),), -0.2, 0.2)), 1.0, 16.0)
    amplitudes = jnp.clip(jnp.exp(math.log(0.6) - 1.3862944 * jax.random.uniform(splits[3], (ATOMS,), jnp.float32) ** level_of(splits[3], (ATOMS,), ((0, 8),), -0.2, 0.2)), 0.15, 0.6)
    charges = jnp.clip(jax.random.uniform(splits[4], (ATOMS,), jnp.float32, -1.2, 1.2) * level_of(splits[4], (ATOMS,), ((0, 8),), -0.4, 0.0), -1.2, 1.2)
    return {"positions": positions, "velocities": velocities, "masses": masses, "amplitudes": amplitudes, "charges": charges}


time_step = 0.05
spring_rate = 25.0
near_scale = 4.0
far_scale = 2.0


def contraction(bead_count, small_count):
    bead_place = jnp.arange(bead_count, dtype=jnp.float32) / bead_count
    small_place = jnp.arange(small_count, dtype=jnp.float32) / small_count
    phase = 2.0 * jnp.pi * (bead_place[None, :] - small_place[:, None])
    modes = jnp.arange(1, small_count // 2, dtype=jnp.float32)
    total = 1.0 + jnp.cos(0.5 * small_count * phase) + 2.0 * jnp.sum(jnp.cos(modes[:, None, None] * phase[None]), axis=0)
    return total / bead_count


def pair_force(targets, sources, target_share, source_share, scale):
    between = targets[..., :, :, None] - sources[..., :, None, :]
    square = jnp.sum(between * between, axis=-3)
    weight = target_share[:, None] * source_share[None, :] * jnp.exp(-0.5 * scale * square) * scale
    return jnp.sum(weight[..., None, :, :] * between, axis=-1)


def field_forces(coords, shares, reach, scale):
    plane_size = PLANE_ATOMS
    planes_total = ATOMS // PLANE_ATOMS
    margin = reach * plane_size
    offset = jnp.concatenate([jnp.full((margin,), -float(planes_total), jnp.float32), jnp.zeros((ATOMS,), jnp.float32), jnp.full((margin,), float(planes_total), jnp.float32)])
    shift = jnp.stack([offset, jnp.zeros_like(offset), jnp.zeros_like(offset)])
    extended = jnp.concatenate([coords[..., -margin:], coords, coords[..., :margin]], axis=-1) + shift
    shares_wide = jnp.concatenate([shares[-margin:], shares, shares[:margin]])
    width = (2 * reach + 1) * plane_size

    def one_plane(plane):
        start = plane * plane_size
        targets = lax.dynamic_slice_in_dim(coords, start, plane_size, 2)
        sources = lax.dynamic_slice_in_dim(extended, start, width, 2)
        target_share = lax.dynamic_slice_in_dim(shares, start, plane_size, 0)
        source_share = lax.dynamic_slice_in_dim(shares_wide, start, width, 0)
        return pair_force(targets, sources, target_share, source_share, scale)

    forces = lax.map(one_plane, jnp.arange(planes_total, dtype=jnp.int32))
    return jnp.transpose(forces, (1, 2, 0, 3)).reshape(coords.shape)


def reference(positions, velocities, masses, amplitudes, charges):
    table = contraction(BEADS, CBEADS)

    def fast(coords):
        springs = 2.0 * coords - jnp.roll(coords, 1, 0) - jnp.roll(coords, -1, 0)
        return field_forces(coords, amplitudes, 1, near_scale) - spring_rate * masses * springs

    def slow(coords):
        contracted = jnp.einsum("cb,bka->cka", table, coords, precision=lax.Precision.HIGHEST)
        far = field_forces(contracted, charges, 2, far_scale)
        return (BEADS / CBEADS) * jnp.einsum("cb,cka->bka", table, far, precision=lax.Precision.HIGHEST)

    inverse = 1.0 / masses
    outer_dt = INNER_STEPS * time_step
    coords = positions
    speeds = velocities
    quick = fast(coords)
    gentle = slow(coords)
    for outer_step in range(OUTER_STEPS):
        speeds = speeds + 0.5 * outer_dt * gentle * inverse
        for inner_step in range(INNER_STEPS):
            speeds = speeds + 0.5 * time_step * quick * inverse
            coords = coords + time_step * speeds
            quick = fast(coords)
            speeds = speeds + 0.5 * time_step * quick * inverse
        gentle = slow(coords)
        speeds = speeds + 0.5 * outer_dt * gentle * inverse
    return coords - positions, speeds
```

```python
import math

import jax
import jax.numpy as jnp
import numpy as np
from jax import lax
from jax.experimental import pallas as pl
from jax.experimental.pallas import tpu as pltpu
from jax.sharding import PartitionSpec as P

INNER_STEPS = 2
OUTER_STEPS = 2
PLANE_ATOMS = 512

time_step = 0.05
spring_rate = 25.0
near_scale = 4.0
far_scale = 2.0

MESH = pl.DeviceIdType.MESH
F32 = jnp.float32
BF16 = jnp.bfloat16
PA = PLANE_ATOMS
PHASES = INNER_STEPS * OUTER_STEPS + 1
EVENTS = OUTER_STEPS + 1
FEATURES = 64
HALF = PA // 2


def contraction(bead_count, small_count):
    bead_place = np.arange(bead_count, dtype=np.float64) / bead_count
    small_place = np.arange(small_count, dtype=np.float64) / small_count
    phase = 2.0 * np.pi * (bead_place[None, :] - small_place[:, None])
    modes = np.arange(1, small_count // 2, dtype=np.float64)
    total = 1.0 + np.cos(0.5 * small_count * phase)
    total = total + 2.0 * np.sum(np.cos(modes[:, None, None] * phase[None]), axis=0)
    return (total / bead_count).astype(np.float32)


def rows_of(width):
    return lax.broadcasted_iota(jnp.int32, (8, width), 0)


def cut(x):
    high = x.astype(BF16).astype(F32)
    rest = x - high
    mid = rest.astype(BF16).astype(F32)
    low = (rest - mid).astype(BF16).astype(F32)
    return high, mid, low


def scaled(x, first_centre, rate):
    quarter = rows_of(x.shape[1]) & 3
    centre = jnp.where(quarter == 0, first_centre, jnp.where(quarter == 3, 0.0, 1.0))
    return (x - centre) * rate


def source_features(z, share):
    quarter = rows_of(z.shape[1]) & 3
    square = 0.5 * z * z
    norm = pltpu.roll(square, 1, 0) + pltpu.roll(square, 2, 0) + pltpu.roll(square, 3, 0)
    high, mid, low = cut(jnp.where(quarter == 3, norm, z))
    one = jnp.ones_like(z)
    features = jnp.concatenate([high, high, mid, mid, high, low, one, jnp.zeros_like(z)], axis=0)
    weighted = share * jnp.where(quarter == 3, 1.0, z)
    first, second, _ = cut(weighted)
    return features.T.astype(BF16), jnp.concatenate([first, second], axis=0).astype(BF16)


def target_features(z):
    quarter = rows_of(z.shape[1]) & 3
    square = 0.5 * z * z
    norm = pltpu.roll(square, 1, 0) + pltpu.roll(square, 2, 0) + pltpu.roll(square, 3, 0)
    high, mid, low = cut(jnp.where(quarter == 3, norm, z))
    flat = quarter == 3
    own = jnp.where(
        flat,
        -high,
        jnp.where(quarter == 2, -pltpu.roll(mid, 7, 0), jnp.where(quarter == 1, -pltpu.roll(low, 6, 0), 0.0)),
    )
    high = jnp.where(flat, -1.0, high)
    mid = jnp.where(flat, 0.0, mid)
    low = jnp.where(flat, 0.0, low)
    return [high, mid, high, mid, low, high, own, jnp.zeros_like(z)]


def masked(groups, half):
    keep = (rows_of(groups[0].shape[1]) >> 2) == half
    return jnp.concatenate([jnp.where(keep, g, 0.0) for g in groups], axis=0).astype(BF16)


def weighted_sum(weighted, weight, pieces, flip):
    dims = (((1,), (1 if flip else 0,)), ((), ()))
    high = weight.astype(BF16)
    total = lax.dot_general(weighted, high, dims, preferred_element_type=F32)
    if pieces == 2:
        rest = (weight - high.astype(F32)).astype(BF16)
        total = total + lax.dot_general(weighted, rest, dims, preferred_element_type=F32)
    return total[:8] + total[8:]


def block_items(sources, weighted, targets, t, kind, others=None):
    items = []
    for h in range(2):
        rows = slice(h * HALF, (h + 1) * HALF)
        width = HALF if kind == "self" and h == 0 else PA
        flips = None
        if kind == "self" and h == 1:
            flips = (weighted, HALF, (t, 1))
        if kind == "cross":
            flips = (others, PA, (1, h))
        items.append((sources, rows, weighted, targets, width, t, flips))
    return items


def run_items(items, pieces):
    waiting = None
    for item, sums_of in list(items) + [(None, None)]:
        exponent = None
        if item is not None:
            sources, rows, _, targets, width = item[:5]
            exponent = jnp.dot(sources[rows, :], targets[:, :width], preferred_element_type=F32)
        if waiting is not None:
            (_, rows, weighted, _, width, t, flips), held, sums = waiting
            weight = jnp.exp2(held)
            direct = weighted_sum(weighted[:, rows], weight, pieces, False)
            for half in range(width // HALF):
                part = direct[:, half * HALF:(half + 1) * HALF]
                sums[t, half] = sums[t, half] + part if (t, half) in sums else part
            if flips is not None:
                shares, depth, key = flips
                part = weighted_sum(shares[:, :depth], weight[:, :depth], pieces, True)
                sums[key] = sums[key] + part if key in sums else part
        waiting = (item, exponent, sums_of)


def forces_of(z, sums):
    quarter = rows_of(z.shape[1]) & 3
    plain = jnp.where(quarter == 3, sums, 0.0)
    spread = pltpu.roll(plain, 7, 0) + pltpu.roll(plain, 6, 0) + pltpu.roll(plain, 5, 0)
    return jnp.where(quarter == 3, 0.0, z * spread - sums)


def kernel(
    nb, ns, planes_total,
    table, pos, vel, mass, amp, chg,
    moved, final,
    X, V, AF, prm, prm_n, halo, ring_p, ring_n,
    pair_s, pair_r, joint, joint_r, Y, far_s, far_r,
    nST, nXS, nT, nG, fST, fXS, fT, fG,
    prm_ss, prm_rs, halo_ss, halo_rs, ring_ss, ring_rs, pair_ss, pair_rs, joint_ss, joint_rs, far_ss, far_rs,
):
    me_b = lax.axis_index("bead")
    me_s = lax.axis_index("slab")
    left_s = lax.rem(me_s + ns - 1, ns)
    right_s = lax.rem(me_s + 1, ns)
    left = (me_b, left_s)
    right = (me_b, right_s)
    prev = (lax.rem(me_b + nb - 1, nb), me_s)
    after = (lax.rem(me_b + 1, nb), me_s)
    chips = nb // 2
    chip = me_b // 2
    core = lax.rem(me_b, 2)
    mate = (2 * chip + 1 - core, me_s)
    pairs = X.shape[1]
    beads_here = 2 * pairs
    atoms = X.shape[3]
    first_bead = me_b * beads_here

    def across(d, which):
        return 2 * lax.rem(chip + d, chips) + which

    def remote(src, dst, ss, rs, to):
        return pltpu.make_async_remote_copy(
            src_ref=src, dst_ref=dst, send_sem=ss, recv_sem=rs, device_id=to, device_id_type=MESH
        )

    barrier = pltpu.get_barrier_semaphore()
    for d in range(chips):
        for side in (left_s, right_s):
            pl.semaphore_signal(barrier, inc=1, device_id=(across(d, core), side), device_id_type=MESH)
    for d in range(1, nb):
        other = (lax.rem(me_b + d, nb), me_s)
        pl.semaphore_signal(barrier, inc=1, device_id=other, device_id_type=MESH)

    X[0] = jnp.zeros((pairs, 8, atoms), F32)
    V[...] = jnp.zeros_like(V)
    for b in range(beads_here):
        p, r = b // 2, 4 * (b % 2)
        for c in range(3):
            X[0, p, r + c:r + c + 1, :] = pos[c, b:b + 1, :]
            V[p, r + c:r + c + 1, :] = vel[c, b:b + 1, :]
    prm[...] = jnp.zeros_like(prm)
    for t in range(2):
        lanes = slice(t * PA, (t + 1) * PA)
        prm[t:t + 1, :] = amp[:, lanes]
        prm[2 + t:3 + t, :] = chg[:, lanes]

    centre = (me_s * 2).astype(F32) + 1.0
    span = float(planes_total)
    centre_l = centre + jnp.where(me_s == 0, span, 0.0)
    centre_r = centre - jnp.where(me_s == ns - 1, span, 0.0)
    near_rate = math.sqrt(near_scale / math.log(2.0))
    far_rate = math.sqrt(far_scale / math.log(2.0))

    inverse = 1.0 / mass[...]

    pl.semaphore_wait(barrier, nb - 1 + 2 * chips)

    prm_copies = [
        remote(prm, prm_n.at[1], prm_ss.at[1], prm_rs.at[1], left),
        remote(prm, prm_n.at[0], prm_ss.at[0], prm_rs.at[0], right),
    ]

    def halo_copies(k):
        return [
            remote(X.at[k, :, :, pl.ds(0, PA)], halo.at[k, 1], halo_ss.at[k, 1], halo_rs.at[k, 1], left),
            remote(X.at[k, :, :, pl.ds(atoms - PA, PA)], halo.at[k, 0], halo_ss.at[k, 0], halo_rs.at[k, 0], right),
        ]

    def halo_from(k, side):
        return remote(X.at[k, :, :, pl.ds(0, PA)], halo.at[k, side], halo_ss.at[k, side], halo_rs.at[k, side], left)

    def ring_copies(k):
        return [
            remote(X.at[k, pairs - 1], ring_p.at[k], ring_ss.at[k, 0], ring_rs.at[k, 0], after),
            remote(X.at[k, 0], ring_n.at[k], ring_ss.at[k, 1], ring_rs.at[k, 1], prev),
        ]

    def far_copies(e):
        return [
            remote(far_s.at[e], far_r.at[e, d], far_ss.at[e, d], far_rs.at[e, d], (lax.rem(me_b + d, nb), me_s))
            for d in range(1, nb)
        ]

    def pair_copy(e):
        return remote(pair_s.at[e], pair_r.at[e], pair_ss.at[e], pair_rs.at[e], mate)

    def joint_copy(e, place, d, to):
        return remote(
            joint.at[e, d], joint_r.at[e, place, d], joint_ss.at[e, place, d], joint_rs.at[e, place, d],
            (across(d, core), to),
        )

    def joint_copies(e):
        return (
            [joint_copy(e, 1, d, left_s) for d in range(chips)]
            + [joint_copy(e, 0, d, right_s) for d in range(chips)]
            + [joint_copy(e, 2, d, me_s) for d in range(1, chips)]
        )

    low_rows = rows_of(PA) < 4

    def partial_of(k, c):
        total = None
        for p in range(pairs):
            first = table[c, first_bead + 2 * p]
            second = table[c, first_bead + 2 * p + 1]
            term = jnp.where(rows_of(atoms) < 4, first, second) * X[k, p]
            total = term if total is None else total + term
        total = total + pltpu.roll(total, 4, 0)
        return jnp.where(low_rows, total[:, :PA], total[:, PA:])

    def far_halves(tile):
        first = jnp.where(low_rows, tile, 0.0)
        second = jnp.where(low_rows, pltpu.roll(tile, 4, 0), 0.0)
        return first, second

    def side_of(j):
        return jnp.where(me_s == 0, 1 - j, j)

    near_own = ((0, 1, "self"), (0, 2, "cross"), (1, 2, "self"))
    far_own = ((0, 2, "self"), (0, 3, "cross"), (1, 3, "self"))

    def near_blocks(p, parts, first):
        sums = ({}, {})
        items = []
        for part in parts:
            for t, q, kind in near_own:
                others = nXS.at[p, 1] if kind == "cross" else None
                block = block_items(nST.at[p, q], nXS.at[p, q], nT.at[p, t, part], t, kind, others)
                items += [(item, sums[part]) for item in block]
        run_items(items, 1)
        top = rows_of(HALF) < 4
        for t, half in sums[parts[0]]:
            lanes = slice(half * HALF, (half + 1) * HALF)
            if len(parts) == 2:
                both = jnp.where(top, sums[0][t, half], sums[1][t, half])
            else:
                both = jnp.where(top == (parts[0] == 0), sums[parts[0]][t, half], 0.0)
            if first:
                nG[p, t, :, lanes] = both
            else:
                nG[p, t, :, lanes] += both

    def near_side(side):
        sums = {}
        items = []
        for p in range(pairs):
            for part in range(2):
                own = sums.setdefault((p, part), {})
                block = block_items(nST.at[p, 3 * side], nXS.at[p, 3 * side], nT.at[p, side, part], 0, "rim")
                items += [(item, own) for item in block]
        run_items(items, 1)
        for p in range(pairs):
            for half in range(2):
                lanes = slice(half * HALF, (half + 1) * HALF)
                both = jnp.where(rows_of(HALF) < 4, sums[p, 0][0, half], sums[p, 1][0, half])
                nG[p, side, :, lanes] += both

    def far_blocks(blocks, first):
        items, sums, places = [], {}, {}
        for label, t, q, kind in blocks:
            others = fXS.at[2] if kind == "cross" else None
            places[label] = t
            block = block_items(fST.at[q], fXS.at[q], fT.at[t], label, kind, others)
            items += [(item, sums) for item in block]
        run_items(items, 2)
        for label, half in sorted(sums):
            lanes = slice(half * HALF, (half + 1) * HALF)
            if first:
                fG[places[label], :, lanes] = sums[label, half]
            else:
                fG[places[label], :, lanes] += sums[label, half]

    def phase(k, carry):
        slow_turn = lax.rem(k, INNER_STEPS) == 0
        e = k // INNER_STEPS

        @pl.when(slow_turn)
        def _():
            for d in range(chips):
                pair_s[e, d] = partial_of(k, across(d, 1 - core))
            pair_copy(e).start()

        @pl.when(k == 0)
        def _():
            for copy in prm_copies:
                copy.start()

        for copy in halo_copies(k) + ring_copies(k):
            copy.start()

        @pl.when(slow_turn)
        def _():
            for d in range(chips):
                joint[e, d] = partial_of(k, across(d, core))

        for p in range(pairs):
            for t in range(2):
                lanes = slice(t * PA, (t + 1) * PA)
                z = scaled(X[k, p, :, lanes], centre, near_rate)
                nST[p, 1 + t], nXS[p, 1 + t] = source_features(z, amp[:, lanes])
                groups = target_features(z)
                nT[p, t, 0] = masked(groups, 0)
                nT[p, t, 1] = masked(groups, 1)

        near_blocks(0, (0,), True)

        @pl.when(slow_turn)
        def _():
            pair_copy(e).wait_recv()
            for d in range(chips):
                joint[e, d] += pair_r[e, d]
            for copy in joint_copies(e):
                copy.start()

        near_blocks(0, (1,), False)

        @pl.loop(1, pairs)
        def _(p):
            near_blocks(p, (0, 1), True)

        @pl.when(k == 0)
        def _():
            for copy in prm_copies:
                copy.wait_recv()

        @pl.when(slow_turn)
        def _():
            total = joint[e, 0]
            for d in range(1, chips):
                joint_copy(e, 2, d, me_s).wait_recv()
                total = total + joint_r[e, 2, d]
            Y[e] = total
            for t, half in enumerate(far_halves(total)):
                z = scaled(half, centre, far_rate)
                z = jnp.where(low_rows, z, 0.0)
                fST[2 + t], fXS[2 + t] = source_features(z, chg[:, t * PA:(t + 1) * PA])
                fT[t] = masked(target_features(z), 0)
            far_blocks([(t, t, q, kind) for t, q, kind in far_own], True)

            @pl.loop(0, 2)
            def _(j):
                side = side_of(j)
                tile = None
                for d in range(chips):
                    joint_copy(e, side, d, left_s).wait_recv()
                    term = joint_r[e, side, d]
                    tile = term if tile is None else tile + term
                middle = jnp.where(side == 0, centre_l, centre_r)
                for t, half in enumerate(far_halves(tile)):
                    z = scaled(half, middle, far_rate)
                    z = jnp.where(low_rows, z, 0.0)
                    fST[4 * side + t], fXS[4 * side + t] = source_features(z, prm_n[side, 2 + t:3 + t, :])
                facing = 1 + 3 * side
                far_blocks([(0, 0, facing, "rim"), (1, 1, facing, "rim"), (2, side, 5 * side, "rim")], False)

            halves = []
            for t, half in enumerate(far_halves(Y[e])):
                lanes = slice(t * PA, (t + 1) * PA)
                z = scaled(half, centre, far_rate)
                coefficient = chg[:, lanes] * (far_scale / far_rate)
                halves.append(coefficient * forces_of(z, fG[t]))
            far_s[e] = jnp.where(low_rows, halves[0], pltpu.roll(halves[1], 4, 0))
            for copy in far_copies(e):
                copy.start()

        @pl.loop(0, 2)
        def _(j):
            side = side_of(j)
            halo_from(k, side).wait_recv()
            middle = jnp.where(side == 0, centre_l, centre_r)
            share = jnp.where(side == 0, prm_n[0, 1:2, :], prm_n[1, 0:1, :])
            for p in range(pairs):
                z = scaled(halo[k, side, p], middle, near_rate)
                nST[p, 3 * side], nXS[p, 3 * side] = source_features(z, share)
            near_side(side)

        for copy in ring_copies(k):
            copy.wait_recv()
        upper = rows_of(atoms) < 4
        rolled = [pltpu.roll(X[k, p], 4, 0) for p in range(pairs)]
        before = [pltpu.roll(ring_p[k], 4, 0)] + rolled
        behind = rolled + [pltpu.roll(ring_n[k], 4, 0)]
        for p in range(pairs):
            springs = 2.0 * X[k, p] - rolled[p] - jnp.where(upper, before[p], behind[p + 1])
            AF[p] = -spring_rate * springs
            for t in range(2):
                lanes = slice(t * PA, (t + 1) * PA)
                z = scaled(X[k, p, :, lanes], centre, near_rate)
                coefficient = amp[:, lanes] * (near_scale / near_rate) * inverse[:, lanes]
                AF[p, :, lanes] += coefficient * forces_of(z, nG[p, t])

        edge = (k == 0) | (k == PHASES - 1)
        fast_step = jnp.where(edge, 0.5 * time_step, time_step)
        slow_step = jnp.where(edge, 0.5 * INNER_STEPS * time_step, INNER_STEPS * time_step)
        for p in range(pairs):
            V[p] += fast_step * AF[p]

        @pl.when(slow_turn)
        def _():
            for copy in far_copies(e):
                copy.wait_recv()
            ratio = float(beads_here)
            total = [[None, None] for _ in range(pairs)]
            for d in range(nb):
                tile = far_s[e] if d == 0 else far_r[e, d]
                c = lax.rem(me_b + nb - d, nb)
                turned = pltpu.roll(tile, 4, 0)
                doubled = (jnp.where(low_rows, tile, turned), jnp.where(low_rows, turned, tile))
                for p in range(pairs):
                    first = table[c, first_bead + 2 * p] * ratio
                    second = table[c, first_bead + 2 * p + 1] * ratio
                    level = jnp.where(low_rows, first, second)
                    for t in range(2):
                        term = level * doubled[t]
                        total[p][t] = term if d == 0 else total[p][t] + term
            for p in range(pairs):
                for t in range(2):
                    lanes = slice(t * PA, (t + 1) * PA)
                    V[p, :, lanes] += slow_step * inverse[:, lanes] * total[p][t]

        @pl.when(k < PHASES - 1)
        def _():
            for p in range(pairs):
                X[k + 1, p] = X[k, p] + time_step * V[p]

        return carry

    lax.fori_loop(0, PHASES, phase, 0)

    last = PHASES - 1
    for b in range(beads_here):
        p, r = b // 2, 4 * (b % 2)
        for c in range(3):
            moved[c, b:b + 1, :] = X[last, p, r + c:r + c + 1, :] - pos[c, b:b + 1, :]
            final[c, b:b + 1, :] = V[p, r + c:r + c + 1, :]

    for copy in prm_copies:
        copy.wait_send()

    @pl.loop(0, PHASES)
    def _(k):
        for copy in halo_copies(k) + ring_copies(k):
            copy.wait_send()

    @pl.loop(0, EVENTS)
    def _(e):
        for copy in [pair_copy(e)] + joint_copies(e) + far_copies(e):
            copy.wait_send()


def solution(mesh):
    nb, ns = mesh.shape["bead"], mesh.shape["slab"]

    def shards(positions, velocities, masses, amplitudes, charges):
        beads_here, _, atoms = positions.shape
        assert atoms == 2 * PA and beads_here % 2 == 0 and nb % 2 == 0 and ns > 2
        pairs = beads_here // 2
        table = jnp.asarray(contraction(beads_here * nb, nb))
        vmem = pl.BlockSpec(memory_space=pltpu.VMEM)
        out = jax.ShapeDtypeStruct((3, beads_here, atoms), F32)
        V, D = pltpu.VMEM, pltpu.SemaphoreType.DMA
        tile = (8, PA)

        def body(*refs):
            kernel(nb, ns, 2 * ns, *refs)

        shifted, speeds = pl.pallas_call(
            body,
            name="rod",
            out_shape=(out, out),
            in_specs=[pl.BlockSpec(memory_space=pltpu.SMEM)] + [vmem] * 5,
            out_specs=(vmem, vmem),
            scratch_shapes=[
                V((PHASES, pairs, 8, atoms), F32),
                V((pairs, 8, atoms), F32),
                V((pairs, 8, atoms), F32),
                V(tile, F32), V((2,) + tile, F32),
                V((PHASES, 2, pairs) + tile, F32),
                V((PHASES, 8, atoms), F32), V((PHASES, 8, atoms), F32),
                V((EVENTS, nb // 2) + tile, F32), V((EVENTS, nb // 2) + tile, F32),
                V((EVENTS, nb // 2) + tile, F32), V((EVENTS, 3, nb // 2) + tile, F32),
                V((EVENTS,) + tile, F32),
                V((EVENTS,) + tile, F32), V((EVENTS, nb) + tile, F32),
                V((pairs, 4, PA, FEATURES), BF16), V((pairs, 4, 16, PA), BF16),
                V((pairs, 2, 2, FEATURES, PA), BF16), V((pairs, 2) + tile, F32),
                V((6, PA, FEATURES), BF16), V((6, 16, PA), BF16),
                V((2, FEATURES, PA), BF16), V((2,) + tile, F32),
                D((2,)), D((2,)), D((PHASES, 2)), D((PHASES, 2)), D((PHASES, 2)), D((PHASES, 2)),
                D((EVENTS,)), D((EVENTS,)), D((EVENTS, 3, nb // 2)), D((EVENTS, 3, nb // 2)),
                D((EVENTS, nb)), D((EVENTS, nb)),
            ],
            compiler_params=pltpu.CompilerParams(collective_id=0, has_side_effects=True),
        )(table, positions.transpose(1, 0, 2), velocities.transpose(1, 0, 2), masses[None], amplitudes[None], charges[None])
        return shifted.transpose(1, 0, 2), speeds.transpose(1, 0, 2)

    both = P("bead", None, "slab")
    return jax.shard_map(
        shards, mesh=mesh, in_specs=(both, both, P("slab"), P("slab"), P("slab")), out_specs=(both, both), check_vma=False
    )
```

```python
import math

import jax
import jax.numpy as jnp
import numpy as np
from jax import lax
from jax.experimental import pallas as pl
from jax.experimental.pallas import tpu as pltpu
from jax.sharding import PartitionSpec as P

INNER_STEPS = 2
OUTER_STEPS = 2
PLANE_ATOMS = 512

time_step = 0.05
spring_rate = 25.0
near_scale = 4.0
far_scale = 2.0

MESH = pl.DeviceIdType.MESH
F32 = jnp.float32
BF16 = jnp.bfloat16
PA = PLANE_ATOMS
PHASES = INNER_STEPS * OUTER_STEPS + 1
EVENTS = OUTER_STEPS + 1
FEATURES = 64
HALF = PA // 2


def contraction(bead_count, small_count):
    bead_place = np.arange(bead_count, dtype=np.float64) / bead_count
    small_place = np.arange(small_count, dtype=np.float64) / small_count
    phase = 2.0 * np.pi * (bead_place[None, :] - small_place[:, None])
    modes = np.arange(1, small_count // 2, dtype=np.float64)
    total = 1.0 + np.cos(0.5 * small_count * phase)
    total = total + 2.0 * np.sum(np.cos(modes[:, None, None] * phase[None]), axis=0)
    return (total / bead_count).astype(np.float32)


def rows_of(width):
    return lax.broadcasted_iota(jnp.int32, (8, width), 0)


def cut(x):
    high = x.astype(BF16).astype(F32)
    rest = x - high
    mid = rest.astype(BF16).astype(F32)
    low = (rest - mid).astype(BF16).astype(F32)
    return high, mid, low


def scaled(x, first_centre, rate):
    quarter = rows_of(x.shape[1]) & 3
    centre = jnp.where(quarter == 0, first_centre, jnp.where(quarter == 3, 0.0, 1.0))
    return (x - centre) * rate


def source_features(z, share):
    quarter = rows_of(z.shape[1]) & 3
    square = 0.5 * z * z
    norm = pltpu.roll(square, 1, 0) + pltpu.roll(square, 2, 0) + pltpu.roll(square, 3, 0)
    high, mid, low = cut(jnp.where(quarter == 3, norm, z))
    one = jnp.ones_like(z)
    features = jnp.concatenate([high, high, mid, mid, high, low, one, jnp.zeros_like(z)], axis=0)
    weighted = share * jnp.where(quarter == 3, 1.0, z)
    first, second, _ = cut(weighted)
    return features.T.astype(BF16), jnp.concatenate([first, second], axis=0).astype(BF16)


def target_features(z):
    quarter = rows_of(z.shape[1]) & 3
    square = 0.5 * z * z
    norm = pltpu.roll(square, 1, 0) + pltpu.roll(square, 2, 0) + pltpu.roll(square, 3, 0)
    high, mid, low = cut(jnp.where(quarter == 3, norm, z))
    flat = quarter == 3
    own = jnp.where(
        flat,
        -high,
        jnp.where(quarter == 2, -pltpu.roll(mid, 7, 0), jnp.where(quarter == 1, -pltpu.roll(low, 6, 0), 0.0)),
    )
    high = jnp.where(flat, -1.0, high)
    mid = jnp.where(flat, 0.0, mid)
    low = jnp.where(flat, 0.0, low)
    return [high, mid, high, mid, low, high, own, jnp.zeros_like(z)]


def masked(groups, half):
    keep = (rows_of(groups[0].shape[1]) >> 2) == half
    return jnp.concatenate([jnp.where(keep, g, 0.0) for g in groups], axis=0).astype(BF16)


def weighted_sum(weighted, weight, pieces, flip):
    dims = (((1,), (1 if flip else 0,)), ((), ()))
    high = weight.astype(BF16)
    total = lax.dot_general(weighted, high, dims, preferred_element_type=F32)
    if pieces == 2:
        rest = (weight - high.astype(F32)).astype(BF16)
        total = total + lax.dot_general(weighted, rest, dims, preferred_element_type=F32)
    return total[:8] + total[8:]


def block_items(sources, weighted, targets, t, kind, sums, pieces, others=None):
    items = []
    for h in range(2):
        rows = slice(h * HALF, (h + 1) * HALF)
        width = HALF if kind == "self" and h == 0 else PA
        flips = None
        if kind == "self" and h == 1:
            flips = (weighted, HALF, (t, 1))
        if kind == "cross":
            flips = (others, PA, (1, h))
        items.append((sources, rows, weighted, targets, width, t, flips, sums, pieces))
    return items


def finish(item, exponent):
    _, rows, weighted, _, width, t, flips, sums, pieces = item
    weight = jnp.exp2(exponent)
    direct = weighted_sum(weighted[:, rows], weight, pieces, False)
    for half in range(width // HALF):
        part = direct[:, half * HALF:(half + 1) * HALF]
        sums[t, half] = sums[t, half] + part if (t, half) in sums else part
    if flips is not None:
        shares, depth, key = flips
        part = weighted_sum(shares[:, :depth], weight[:, :depth], pieces, True)
        sums[key] = sums[key] + part if key in sums else part


def run_stream(entries):
    waiting, pending = None, []
    for entry in entries:
        if not isinstance(entry, tuple):
            entry()
            continue
        if entry[0] == "then":
            pending.append(entry[1])
            continue
        sources, rows, _, targets, width = entry[:5]
        exponent = jnp.dot(sources[rows, :], targets[:, :width], preferred_element_type=F32)
        if waiting is not None:
            finish(*waiting)
        for act in pending:
            act()
        waiting, pending = (entry, exponent), []
    finish(*waiting)
    for act in pending:
        act()


def forces_of(z, sums):
    quarter = rows_of(z.shape[1]) & 3
    plain = jnp.where(quarter == 3, sums, 0.0)
    spread = pltpu.roll(plain, 7, 0) + pltpu.roll(plain, 6, 0) + pltpu.roll(plain, 5, 0)
    return jnp.where(quarter == 3, 0.0, z * spread - sums)


def kernel(
    nb, ns, planes_total,
    table_h, pos_h, vel_h, mass_h, amp_h, chg_h,
    moved, final,
    table, pos, vel, mass, amp, chg, in_sem,
    X, V, AF, prm, prm_n, halo, ring_p, ring_n,
    pair_s, pair_r, joint, joint_r, Y, far_s, far_r,
    nST, nXS, nT, nG, fST, fXS, fT, fG,
    prm_ss, prm_rs, halo_ss, halo_rs, ring_ss, ring_rs, pair_ss, pair_rs, joint_ss, joint_rs, far_ss, far_rs,
):
    me_b = lax.axis_index("bead")
    me_s = lax.axis_index("slab")
    left_s = lax.rem(me_s + ns - 1, ns)
    right_s = lax.rem(me_s + 1, ns)
    left = (me_b, left_s)
    right = (me_b, right_s)
    prev = (lax.rem(me_b + nb - 1, nb), me_s)
    after = (lax.rem(me_b + 1, nb), me_s)
    chips = nb // 2
    chip = me_b // 2
    core = lax.rem(me_b, 2)
    mate = (2 * chip + 1 - core, me_s)
    pairs = X.shape[1]
    beads_here = 2 * pairs
    atoms = X.shape[3]
    first_bead = me_b * beads_here

    def across(d, which):
        return 2 * lax.rem(chip + d, chips) + which

    def remote(src, dst, ss, rs, to):
        return pltpu.make_async_remote_copy(
            src_ref=src, dst_ref=dst, send_sem=ss, recv_sem=rs, device_id=to, device_id_type=MESH
        )

    barrier = pltpu.get_barrier_semaphore()
    for d in range(chips):
        for side in (left_s, right_s):
            pl.semaphore_signal(barrier, inc=1, device_id=(across(d, core), side), device_id_type=MESH)
    for d in range(1, nb):
        other = (lax.rem(me_b + d, nb), me_s)
        pl.semaphore_signal(barrier, inc=1, device_id=other, device_id_type=MESH)

    loads = [
        pltpu.make_async_copy(src, dst, in_sem.at[i])
        for i, (src, dst) in enumerate(
            ((pos_h, pos), (vel_h, vel), (amp_h, amp), (chg_h, chg), (mass_h, mass), (table_h, table))
        )
    ]
    for load in loads:
        load.start()
    X[0] = jnp.zeros((pairs, 8, atoms), F32)
    V[...] = jnp.zeros_like(V)
    for load in loads:
        load.wait()
    for b in range(beads_here):
        p, r = b // 2, 4 * (b % 2)
        for c in range(3):
            X[0, p, r + c:r + c + 1, :] = pos[c, b:b + 1, :]
            V[p, r + c:r + c + 1, :] = vel[c, b:b + 1, :]
    prm[...] = jnp.zeros_like(prm)
    for t in range(2):
        lanes = slice(t * PA, (t + 1) * PA)
        prm[t:t + 1, :] = amp[:, lanes]
        prm[2 + t:3 + t, :] = chg[:, lanes]

    centre = (me_s * 2).astype(F32) + 1.0
    span = float(planes_total)
    centre_l = centre + jnp.where(me_s == 0, span, 0.0)
    centre_r = centre - jnp.where(me_s == ns - 1, span, 0.0)
    near_rate = math.sqrt(near_scale / math.log(2.0))
    far_rate = math.sqrt(far_scale / math.log(2.0))

    inverse = 1.0 / mass[...]

    pl.semaphore_wait(barrier, nb - 1 + 2 * chips)

    def prm_copy(e, side, to):
        return remote(prm, prm_n.at[e, side], prm_ss.at[e, side], prm_rs.at[e, side], to)

    def prm_copies(e):
        return [prm_copy(e, 1, left), prm_copy(e, 0, right)]

    def halo_copies(k):
        return [
            remote(X.at[k, :, :, pl.ds(0, PA)], halo.at[k, 1], halo_ss.at[k, 1], halo_rs.at[k, 1], left),
            remote(X.at[k, :, :, pl.ds(atoms - PA, PA)], halo.at[k, 0], halo_ss.at[k, 0], halo_rs.at[k, 0], right),
        ]

    def halo_from(k, side):
        return remote(X.at[k, :, :, pl.ds(0, PA)], halo.at[k, side], halo_ss.at[k, side], halo_rs.at[k, side], left)

    def ring_copies(k):
        return [
            remote(X.at[k, pairs - 1], ring_p.at[k], ring_ss.at[k, 0], ring_rs.at[k, 0], after),
            remote(X.at[k, 0], ring_n.at[k], ring_ss.at[k, 1], ring_rs.at[k, 1], prev),
        ]

    def far_copies(e):
        return [
            remote(far_s.at[e], far_r.at[e, d], far_ss.at[e, d], far_rs.at[e, d], (lax.rem(me_b + d, nb), me_s))
            for d in range(1, nb)
        ]

    def pair_copy(e):
        return remote(pair_s.at[e], pair_r.at[e], pair_ss.at[e], pair_rs.at[e], mate)

    def joint_copy(e, place, d, to):
        return remote(
            joint.at[e, d], joint_r.at[e, place, d], joint_ss.at[e, place, d], joint_rs.at[e, place, d],
            (across(d, core), to),
        )

    def joint_copies(e):
        return (
            [joint_copy(e, 2, d, me_s) for d in range(1, chips)]
            + [joint_copy(e, 1, d, left_s) for d in range(chips)]
            + [joint_copy(e, 0, d, right_s) for d in range(chips)]
        )

    low_rows = rows_of(PA) < 4

    def partial_of(k, c):
        total = None
        for p in range(pairs):
            first = table[c, first_bead + 2 * p]
            second = table[c, first_bead + 2 * p + 1]
            term = jnp.where(rows_of(atoms) < 4, first, second) * X[k, p]
            total = term if total is None else total + term
        total = total + pltpu.roll(total, 4, 0)
        return jnp.where(low_rows, total[:, :PA], total[:, PA:])

    def far_halves(tile):
        first = jnp.where(low_rows, tile, 0.0)
        second = jnp.where(low_rows, pltpu.roll(tile, 4, 0), 0.0)
        return first, second

    def side_of(j):
        return jnp.where(me_s == 0, 1 - j, j)

    near_own = ((0, 1, "self"), (0, 2, "cross"), (1, 2, "self"))
    far_own = ((0, 2, "self"), (0, 3, "cross"), (1, 3, "self"))

    def near_own_items(p, part, sums):
        items = []
        for t, q, kind in near_own:
            others = nXS.at[p, 1] if kind == "cross" else None
            items += block_items(nST.at[p, q], nXS.at[p, q], nT.at[p, t, part], t, kind, sums, 1, others)
        return items

    def far_items(blocks, sums):
        items = []
        for label, t, q, kind in blocks:
            others = fXS.at[2] if kind == "cross" else None
            items += block_items(fST.at[q], fXS.at[q], fT.at[t], label, kind, sums, 2, others)
        return items

    def near_store(p, sums):
        def act():
            for t, half in sums[0]:
                lanes = slice(half * HALF, (half + 1) * HALF)
                nG[p, t, :, lanes] = jnp.where(rows_of(HALF) < 4, sums[0][t, half], sums[1][t, half])
        return act

    def near_add(p, side, sums):
        def act():
            for half in range(2):
                lanes = slice(half * HALF, (half + 1) * HALF)
                nG[p, side, :, lanes] += jnp.where(rows_of(HALF) < 4, sums[0][0, half], sums[1][0, half])
        return act

    def far_store(places, sums, first):
        def act():
            for label, half in sorted(sums):
                lanes = slice(half * HALF, (half + 1) * HALF)
                if first:
                    fG[places[label], :, lanes] = sums[label, half]
                else:
                    fG[places[label], :, lanes] += sums[label, half]
        return act

    def own_features(k):
        for p in range(pairs):
            for t in range(2):
                lanes = slice(t * PA, (t + 1) * PA)
                z = scaled(X[k, p, :, lanes], centre, near_rate)
                nST[p, 1 + t], nXS[p, 1 + t] = source_features(z, amp[:, lanes])
                groups = target_features(z)
                nT[p, t, 0] = masked(groups, 0)
                nT[p, t, 1] = masked(groups, 1)

    def own_entries(after_first):
        entries = []
        for p in range(pairs):
            sums = ({}, {})
            for part in range(2):
                entries += near_own_items(p, part, sums[part])
                if p == 0 and part == 0 and after_first is not None:
                    entries.append(after_first)
            entries.append(("then", near_store(p, sums)))
        return entries

    def rim_ready(k, e, j):
        side = side_of(j)

        def act():
            halo_from(k, side).wait_recv()
            middle = jnp.where(side == 0, centre_l, centre_r)
            share = jnp.where(side == 0, prm_n[e, side, 1:2, :], prm_n[e, side, 0:1, :])
            for p in range(pairs):
                z = scaled(halo[k, side, p], middle, near_rate)
                nST[p, 3 * side], nXS[p, 3 * side] = source_features(z, share)

        return act

    def rim_entries(j):
        side = side_of(j)
        entries = []
        for p in range(pairs):
            sums = ({}, {})
            for part in range(2):
                entries += block_items(
                    nST.at[p, 3 * side], nXS.at[p, 3 * side], nT.at[p, side, part], 0, "rim", sums[part], 1
                )
            entries.append(("then", near_add(p, side, sums)))
        return entries

    def springs(k):
        for copy in ring_copies(k):
            copy.wait_recv()
        upper = rows_of(atoms) < 4
        rolled = [pltpu.roll(X[k, p], 4, 0) for p in range(pairs)]
        before = [pltpu.roll(ring_p[k], 4, 0)] + rolled
        behind = rolled + [pltpu.roll(ring_n[k], 4, 0)]
        for p in range(pairs):
            bends = 2.0 * X[k, p] - rolled[p] - jnp.where(upper, before[p], behind[p + 1])
            AF[p] = -spring_rate * bends

    def kick(k, fast_step):
        for p in range(pairs):
            for t in range(2):
                lanes = slice(t * PA, (t + 1) * PA)
                z = scaled(X[k, p, :, lanes], centre, near_rate)
                coefficient = amp[:, lanes] * (near_scale / near_rate) * inverse[:, lanes]
                V[p, :, lanes] += fast_step * (AF[p, :, lanes] + coefficient * forces_of(z, nG[p, t]))

    def drift(k):
        for p in range(pairs):
            X[k + 1, p] = X[k, p] + time_step * V[p]

    def fast_phase(k):
        for copy in halo_copies(k) + ring_copies(k):
            copy.start()
        own_features(k)
        e = k // INNER_STEPS
        entries = own_entries(None) + [lambda: springs(k), rim_ready(k, e, 0)] + rim_entries(0)
        run_stream(entries + [rim_ready(k, e, 1)] + rim_entries(1))
        kick(k, time_step)
        drift(k)

    def slow_phase(e):
        k = INNER_STEPS * e
        for d in range(chips):
            pair_s[e, d] = partial_of(k, across(d, 1 - core))
        pair_copy(e).start()
        for copy in halo_copies(k) + ring_copies(k) + prm_copies(e):
            copy.start()
        for d in range(chips):
            joint[e, d] = partial_of(k, across(d, core))
        own_features(k)

        def send_joint():
            pair_copy(e).wait_recv()
            for d in range(chips):
                joint[e, d] += pair_r[e, d]
            for copy in joint_copies(e):
                copy.start()

        def own_plane():
            total = joint[e, 0]
            for d in range(1, chips):
                joint_copy(e, 2, d, me_s).wait_recv()
                total = total + joint_r[e, 2, d]
            Y[e] = total
            for t, half in enumerate(far_halves(total)):
                z = scaled(half, centre, far_rate)
                z = jnp.where(low_rows, z, 0.0)
                fST[2 + t], fXS[2 + t] = source_features(z, chg[:, t * PA:(t + 1) * PA])
                fT[t] = masked(target_features(z), 0)

        def send_far():
            halves = []
            for t, half in enumerate(far_halves(Y[e])):
                lanes = slice(t * PA, (t + 1) * PA)
                z = scaled(half, centre, far_rate)
                coefficient = chg[:, lanes] * (far_scale / far_rate)
                halves.append(coefficient * forces_of(z, fG[t]))
            far_s[e] = jnp.where(low_rows, halves[0], pltpu.roll(halves[1], 4, 0))
            for copy in far_copies(e):
                copy.start()

        sums = {}
        entries = own_entries(send_joint) + [lambda: springs(k), own_plane]
        entries += far_items([(t, t, q, kind) for t, q, kind in far_own], sums)
        entries.append(("then", far_store({0: 0, 1: 1}, sums, True)))
        for j in range(2):
            side = side_of(j)

            def facing_plane(side=side):
                tile = None
                for d in range(chips):
                    joint_copy(e, side, d, left_s).wait_recv()
                    term = joint_r[e, side, d]
                    tile = term if tile is None else tile + term
                prm_copy(e, side, left).wait_recv()
                middle = jnp.where(side == 0, centre_l, centre_r)
                for t, half in enumerate(far_halves(tile)):
                    z = scaled(half, middle, far_rate)
                    z = jnp.where(low_rows, z, 0.0)
                    fST[4 * side + t], fXS[4 * side + t] = source_features(z, prm_n[e, side, 2 + t:3 + t, :])

            entries.append(facing_plane)
            sums = {}
            facing = 1 + 3 * side
            entries += far_items([(0, 0, facing, "rim"), (1, 1, facing, "rim"), (2, side, 5 * side, "rim")], sums)
            entries.append(("then", far_store({0: 0, 1: 1, 2: side}, sums, False)))
            entries.append(rim_ready(k, e, j))
        entries.append(("then", send_far))
        entries += rim_entries(0) + rim_entries(1)

        run_stream(entries)

        edge = (e == 0) | (e == EVENTS - 1)
        kick(k, jnp.where(edge, 0.5 * time_step, time_step))
        slow_step = jnp.where(edge, 0.5 * INNER_STEPS * time_step, INNER_STEPS * time_step)
        for copy in far_copies(e):
            copy.wait_recv()
        ratio = float(beads_here)
        total = [[None, None] for _ in range(pairs)]
        for d in range(nb):
            tile = far_s[e] if d == 0 else far_r[e, d]
            c = lax.rem(me_b + nb - d, nb)
            turned = pltpu.roll(tile, 4, 0)
            doubled = (jnp.where(low_rows, tile, turned), jnp.where(low_rows, turned, tile))
            for p in range(pairs):
                first = table[c, first_bead + 2 * p] * ratio
                second = table[c, first_bead + 2 * p + 1] * ratio
                level = jnp.where(low_rows, first, second)
                for t in range(2):
                    term = level * doubled[t]
                    total[p][t] = term if d == 0 else total[p][t] + term
        for p in range(pairs):
            for t in range(2):
                lanes = slice(t * PA, (t + 1) * PA)
                V[p, :, lanes] += slow_step * inverse[:, lanes] * total[p][t]

    def outer(e, carry):
        slow_phase(e)

        @pl.when(e < OUTER_STEPS)
        def _():
            drift(INNER_STEPS * e)

            @pl.loop(1, INNER_STEPS)
            def _(i):
                fast_phase(INNER_STEPS * e + i)

        return carry

    lax.fori_loop(0, EVENTS, outer, 0)

    last = PHASES - 1
    for b in range(beads_here):
        p, r = b // 2, 4 * (b % 2)
        for c in range(3):
            moved[c, b:b + 1, :] = X[last, p, r + c:r + c + 1, :] - pos[c, b:b + 1, :]
            final[c, b:b + 1, :] = V[p, r + c:r + c + 1, :]

    @pl.loop(0, PHASES)
    def _(k):
        for copy in halo_copies(k) + ring_copies(k):
            copy.wait_send()

    @pl.loop(0, EVENTS)
    def _(e):
        for copy in prm_copies(e) + [pair_copy(e)] + joint_copies(e) + far_copies(e):
            copy.wait_send()


def solution(mesh):
    nb, ns = mesh.shape["bead"], mesh.shape["slab"]

    def shards(positions, velocities, masses, amplitudes, charges):
        beads_here, _, atoms = positions.shape
        assert atoms == 2 * PA and beads_here % 2 == 0 and nb % 2 == 0 and ns > 2
        pairs = beads_here // 2
        table = jnp.asarray(contraction(beads_here * nb, nb))
        vmem = pl.BlockSpec(memory_space=pltpu.VMEM)
        out = jax.ShapeDtypeStruct((3, beads_here, atoms), F32)
        V, D = pltpu.VMEM, pltpu.SemaphoreType.DMA
        tile = (8, PA)

        def body(*refs):
            kernel(nb, ns, 2 * ns, *refs)

        shifted, speeds = pl.pallas_call(
            body,
            name="rod",
            out_shape=(pltpu.VMEM(out.shape, F32), pltpu.VMEM(out.shape, F32)),
            in_specs=[pl.BlockSpec(memory_space=pl.ANY)] * 6,
            out_specs=(vmem, vmem),
            scratch_shapes=[
                pltpu.SMEM(table.shape, F32), V(out.shape, F32), V(out.shape, F32),
                V((1, atoms), F32), V((1, atoms), F32), V((1, atoms), F32), D((6,)),
                V((PHASES, pairs, 8, atoms), F32),
                V((pairs, 8, atoms), F32),
                V((pairs, 8, atoms), F32),
                V(tile, F32), V((EVENTS, 2) + tile, F32),
                V((PHASES, 2, pairs) + tile, F32),
                V((PHASES, 8, atoms), F32), V((PHASES, 8, atoms), F32),
                V((EVENTS, nb // 2) + tile, F32), V((EVENTS, nb // 2) + tile, F32),
                V((EVENTS, nb // 2) + tile, F32), V((EVENTS, 3, nb // 2) + tile, F32),
                V((EVENTS,) + tile, F32),
                V((EVENTS,) + tile, F32), V((EVENTS, nb) + tile, F32),
                V((pairs, 4, PA, FEATURES), BF16), V((pairs, 4, 16, PA), BF16),
                V((pairs, 2, 2, FEATURES, PA), BF16), V((pairs, 2) + tile, F32),
                V((6, PA, FEATURES), BF16), V((6, 16, PA), BF16),
                V((2, FEATURES, PA), BF16), V((2,) + tile, F32),
                D((EVENTS, 2)), D((EVENTS, 2)), D((PHASES, 2)), D((PHASES, 2)), D((PHASES, 2)), D((PHASES, 2)),
                D((EVENTS,)), D((EVENTS,)), D((EVENTS, 3, nb // 2)), D((EVENTS, 3, nb // 2)),
                D((EVENTS, nb)), D((EVENTS, nb)),
            ],
            compiler_params=pltpu.CompilerParams(collective_id=0, has_side_effects=True),
        )(table, positions.transpose(1, 0, 2), velocities.transpose(1, 0, 2), masses[None], amplitudes[None], charges[None])
        return shifted.transpose(1, 0, 2), speeds.transpose(1, 0, 2)

    both = P("bead", None, "slab")
    return jax.shard_map(
        shards, mesh=mesh, in_specs=(both, both, P("slab"), P("slab"), P("slab")), out_specs=(both, both), check_vma=False
    )
```

```python
import math

import jax
import jax.numpy as jnp
import numpy as np
from jax import lax
from jax.experimental import pallas as pl
from jax.experimental.pallas import tpu as pltpu
from jax.sharding import PartitionSpec as P

INNER_STEPS = 2
OUTER_STEPS = 2
PLANE_ATOMS = 512

time_step = 0.05
spring_rate = 25.0
near_scale = 4.0
far_scale = 2.0

MESH = pl.DeviceIdType.MESH
F32 = jnp.float32
BF16 = jnp.bfloat16
PA = PLANE_ATOMS
PHASES = INNER_STEPS * OUTER_STEPS + 1
EVENTS = OUTER_STEPS + 1
FEATURES = 64
HALF = PA // 2


def contraction(bead_count, small_count):
    bead_place = np.arange(bead_count, dtype=np.float64) / bead_count
    small_place = np.arange(small_count, dtype=np.float64) / small_count
    phase = 2.0 * np.pi * (bead_place[None, :] - small_place[:, None])
    modes = np.arange(1, small_count // 2, dtype=np.float64)
    total = 1.0 + np.cos(0.5 * small_count * phase)
    total = total + 2.0 * np.sum(np.cos(modes[:, None, None] * phase[None]), axis=0)
    return (total / bead_count).astype(np.float32)


def rows_of(width):
    return lax.broadcasted_iota(jnp.int32, (8, width), 0)


def cut(x):
    high = x.astype(BF16).astype(F32)
    rest = x - high
    mid = rest.astype(BF16).astype(F32)
    low = (rest - mid).astype(BF16).astype(F32)
    return high, mid, low


def scaled(x, first_centre, rate):
    quarter = rows_of(x.shape[1]) & 3
    centre = jnp.where(quarter == 0, first_centre, jnp.where(quarter == 3, 0.0, 1.0))
    return (x - centre) * rate


def source_features(z, share):
    quarter = rows_of(z.shape[1]) & 3
    square = 0.5 * z * z
    norm = pltpu.roll(square, 1, 0) + pltpu.roll(square, 2, 0) + pltpu.roll(square, 3, 0)
    high, mid, low = cut(jnp.where(quarter == 3, norm, z))
    one = jnp.ones_like(z)
    features = jnp.concatenate([high, high, mid, mid, high, low, one, jnp.zeros_like(z)], axis=0)
    weighted = share * jnp.where(quarter == 3, 1.0, z)
    first, second, _ = cut(weighted)
    return features.T.astype(BF16), jnp.concatenate([first, second], axis=0).astype(BF16)


def target_features(z):
    quarter = rows_of(z.shape[1]) & 3
    square = 0.5 * z * z
    norm = pltpu.roll(square, 1, 0) + pltpu.roll(square, 2, 0) + pltpu.roll(square, 3, 0)
    high, mid, low = cut(jnp.where(quarter == 3, norm, z))
    flat = quarter == 3
    own = jnp.where(
        flat,
        -high,
        jnp.where(quarter == 2, -pltpu.roll(mid, 7, 0), jnp.where(quarter == 1, -pltpu.roll(low, 6, 0), 0.0)),
    )
    high = jnp.where(flat, -1.0, high)
    mid = jnp.where(flat, 0.0, mid)
    low = jnp.where(flat, 0.0, low)
    return [high, mid, high, mid, low, high, own, jnp.zeros_like(z)]


def masked(groups, half):
    keep = (rows_of(groups[0].shape[1]) >> 2) == half
    return jnp.concatenate([jnp.where(keep, g, 0.0) for g in groups], axis=0).astype(BF16)


def weighted_sum(weighted, weight, pieces, flip):
    dims = (((1,), (1 if flip else 0,)), ((), ()))
    high = weight.astype(BF16)
    total = lax.dot_general(weighted, high, dims, preferred_element_type=F32)
    if pieces == 2:
        rest = (weight - high.astype(F32)).astype(BF16)
        total = total + lax.dot_general(weighted, rest, dims, preferred_element_type=F32)
    return total[:8] + total[8:]


def block_items(sources, weighted, targets, t, kind, sums, pieces, others=None):
    items = []
    for h in range(2):
        rows = slice(h * HALF, (h + 1) * HALF)
        width = HALF if kind == "self" and h == 0 else PA
        flips = None
        if kind == "self" and h == 1:
            flips = (weighted, HALF, (t, 1))
        if kind == "cross":
            flips = (others, PA, (1, h))
        items.append((sources, rows, weighted, targets, width, t, flips, sums, pieces))
    return items


def finish(item, exponent):
    _, rows, weighted, _, width, t, flips, sums, pieces = item
    weight = jnp.exp2(exponent)
    direct = weighted_sum(weighted[:, rows], weight, pieces, False)
    for half in range(width // HALF):
        part = direct[:, half * HALF:(half + 1) * HALF]
        sums[t, half] = sums[t, half] + part if (t, half) in sums else part
    if flips is not None:
        shares, depth, key = flips
        part = weighted_sum(shares[:, :depth], weight[:, :depth], pieces, True)
        sums[key] = sums[key] + part if key in sums else part


def run_stream(entries):
    waiting, pending = None, []
    for entry in entries:
        if not isinstance(entry, tuple):
            entry()
            continue
        if entry[0] == "then":
            pending.append(entry[1])
            continue
        sources, rows, _, targets, width = entry[:5]
        exponent = jnp.dot(sources[rows, :], targets[:, :width], preferred_element_type=F32)
        if waiting is not None:
            finish(*waiting)
        for act in pending:
            act()
        waiting, pending = (entry, exponent), []
    finish(*waiting)
    for act in pending:
        act()


def forces_of(z, sums):
    quarter = rows_of(z.shape[1]) & 3
    plain = jnp.where(quarter == 3, sums, 0.0)
    spread = pltpu.roll(plain, 7, 0) + pltpu.roll(plain, 6, 0) + pltpu.roll(plain, 5, 0)
    return jnp.where(quarter == 3, 0.0, z * spread - sums)


def kernel(
    nb, ns, planes_total,
    table_h, pos_h, vel_h, mass_h, amp_h, chg_h,
    moved, final,
    table, pos, vel, mass, amp, chg, in_sem,
    X, V, AF, halo, ring_p, ring_n,
    pair_s, pair_r, own_s, part_r, joint, joint_r, Y, far_s, far_r,
    nST, nXS, nT, nG, fST, fXS, fT, fG,
    halo_ss, halo_rs, ring_ss, ring_rs, pair_ss, pair_rs, part_ss, part_rs, joint_ss, joint_rs, far_ss, far_rs,
):
    me_b = lax.axis_index("bead")
    me_s = lax.axis_index("slab")
    left_s = lax.rem(me_s + ns - 1, ns)
    right_s = lax.rem(me_s + 1, ns)
    left = (me_b, left_s)
    right = (me_b, right_s)
    prev = (lax.rem(me_b + nb - 1, nb), me_s)
    after = (lax.rem(me_b + 1, nb), me_s)
    chips = nb // 2
    chip = me_b // 2
    core = lax.rem(me_b, 2)
    mate = (2 * chip + 1 - core, me_s)
    pairs = X.shape[1]
    beads_here = 2 * pairs
    atoms = X.shape[3]
    first_bead = me_b * beads_here

    def across(d, which):
        return 2 * lax.rem(chip + d, chips) + which

    def remote(src, dst, ss, rs, to):
        return pltpu.make_async_remote_copy(
            src_ref=src, dst_ref=dst, send_sem=ss, recv_sem=rs, device_id=to, device_id_type=MESH
        )

    barrier = pltpu.get_barrier_semaphore()
    for d in range(chips):
        for side in (left_s, right_s):
            pl.semaphore_signal(barrier, inc=1, device_id=(across(d, core), side), device_id_type=MESH)
    for d in range(1, nb):
        other = (lax.rem(me_b + d, nb), me_s)
        pl.semaphore_signal(barrier, inc=1, device_id=other, device_id_type=MESH)

    loads = [
        pltpu.make_async_copy(src, dst, in_sem.at[i])
        for i, (src, dst) in enumerate(
            ((pos_h, pos), (vel_h, vel), (amp_h, amp), (chg_h, chg), (mass_h, mass), (table_h, table))
        )
    ]
    for load in loads:
        load.start()
    X[0] = jnp.zeros((pairs, 8, atoms), F32)
    V[...] = jnp.zeros_like(V)
    for load in loads:
        load.wait()
    for b in range(beads_here):
        p, r = b // 2, 4 * (b % 2)
        for c in range(3):
            X[0, p, r + c:r + c + 1, :] = pos[c, b:b + 1, :]
            V[p, r + c:r + c + 1, :] = vel[c, b:b + 1, :]
    for p in range(pairs):
        for r in (3, 7):
            X[0, p, r:r + 1, :] = amp[...]
    quarter = rows_of(PA) & 3
    charges = jnp.where(rows_of(PA) < 4, chg[:, :PA], chg[:, PA:])

    centre = (me_s * 2).astype(F32) + 1.0
    span = float(planes_total)
    centre_l = centre + jnp.where(me_s == 0, span, 0.0)
    centre_r = centre - jnp.where(me_s == ns - 1, span, 0.0)
    near_rate = math.sqrt(near_scale / math.log(2.0))
    far_rate = math.sqrt(far_scale / math.log(2.0))

    inverse = 1.0 / mass[...]

    pl.semaphore_wait(barrier, nb - 1 + 2 * chips)

    def halo_copies(k):
        return [
            remote(X.at[k, :, :, pl.ds(0, PA)], halo.at[k, 1], halo_ss.at[k, 1], halo_rs.at[k, 1], left),
            remote(X.at[k, :, :, pl.ds(atoms - PA, PA)], halo.at[k, 0], halo_ss.at[k, 0], halo_rs.at[k, 0], right),
        ]

    def halo_from(k, side):
        return remote(X.at[k, :, :, pl.ds(0, PA)], halo.at[k, side], halo_ss.at[k, side], halo_rs.at[k, side], left)

    def ring_copies(k):
        return [
            remote(X.at[k, pairs - 1], ring_p.at[k], ring_ss.at[k, 0], ring_rs.at[k, 0], after),
            remote(X.at[k, 0], ring_n.at[k], ring_ss.at[k, 1], ring_rs.at[k, 1], prev),
        ]

    def far_copies(e):
        return [
            remote(far_s.at[e], far_r.at[e, d], far_ss.at[e, d], far_rs.at[e, d], (lax.rem(me_b + d, nb), me_s))
            for d in range(1, nb)
        ]

    def pair_copy(e):
        return remote(pair_s.at[e], pair_r.at[e], pair_ss.at[e], pair_rs.at[e], mate)

    def joint_copy(e, place, d, to):
        return remote(
            joint.at[e, d], joint_r.at[e, place, d], joint_ss.at[e, place, d], joint_rs.at[e, place, d],
            (across(d, core), to),
        )

    def part_copy(e, d, which):
        src = own_s if which == 0 else pair_s
        return remote(
            src.at[e, d], part_r.at[e, d, which], part_ss.at[e, d, which], part_rs.at[e, d, which],
            (across(d, core if which == 0 else 1 - core), me_s),
        )

    def part_copies(e):
        return [part_copy(e, d, which) for d in range(1, chips) for which in range(2)]

    def joint_copies(e):
        return (
            [joint_copy(e, 1, d, left_s) for d in range(chips)]
            + [joint_copy(e, 0, d, right_s) for d in range(chips)]
        )

    low_rows = rows_of(PA) < 4

    def partial_of(k, c):
        total = None
        for p in range(pairs):
            first = table[c, first_bead + 2 * p]
            second = table[c, first_bead + 2 * p + 1]
            term = jnp.where(rows_of(atoms) < 4, first, second) * X[k, p]
            total = term if total is None else total + term
        total = total + pltpu.roll(total, 4, 0)
        return jnp.where(low_rows, total[:, :PA], total[:, PA:])

    def far_halves(tile):
        first = jnp.where(low_rows, tile, 0.0)
        second = jnp.where(low_rows, pltpu.roll(tile, 4, 0), 0.0)
        return first, second

    def side_of(j):
        return jnp.where(me_s == 0, 1 - j, j)

    near_own = ((0, 1, "self"), (0, 2, "cross"), (1, 2, "self"))
    far_own = ((0, 2, "self"), (0, 3, "cross"), (1, 3, "self"))

    def near_own_items(p, part, sums):
        items = []
        for t, q, kind in near_own:
            others = nXS.at[p, 1] if kind == "cross" else None
            items += block_items(nST.at[p, q], nXS.at[p, q], nT.at[p, t, part], t, kind, sums, 1, others)
        return items

    def far_items(blocks, sums):
        items = []
        for label, t, q, kind in blocks:
            others = fXS.at[2] if kind == "cross" else None
            items += block_items(fST.at[q], fXS.at[q], fT.at[t], label, kind, sums, 2, others)
        return items

    def near_store(p, sums):
        def act():
            for t, half in sums[0]:
                lanes = slice(half * HALF, (half + 1) * HALF)
                nG[p, t, :, lanes] = jnp.where(rows_of(HALF) < 4, sums[0][t, half], sums[1][t, half])
        return act

    def near_add(p, side, sums):
        def act():
            for half in range(2):
                lanes = slice(half * HALF, (half + 1) * HALF)
                nG[p, side, :, lanes] += jnp.where(rows_of(HALF) < 4, sums[0][0, half], sums[1][0, half])
        return act

    def far_store(places, sums, first):
        def act():
            for label, half in sorted(sums):
                lanes = slice(half * HALF, (half + 1) * HALF)
                if first:
                    fG[places[label], :, lanes] = sums[label, half]
                else:
                    fG[places[label], :, lanes] += sums[label, half]
        return act

    def own_features(k):
        for p in range(pairs):
            for t in range(2):
                lanes = slice(t * PA, (t + 1) * PA)
                z = scaled(X[k, p, :, lanes], centre, near_rate)
                nST[p, 1 + t], nXS[p, 1 + t] = source_features(z, amp[:, lanes])
                groups = target_features(z)
                nT[p, t, 0] = masked(groups, 0)
                nT[p, t, 1] = masked(groups, 1)

    def own_entries(after_first):
        entries = []
        for p in range(pairs):
            sums = ({}, {})
            for part in range(2):
                entries += near_own_items(p, part, sums[part])
                if p == 0 and part == 0 and after_first is not None:
                    entries.append(after_first)
            entries.append(("then", near_store(p, sums)))
        return entries

    def rim_ready(k, j):
        side = side_of(j)

        def act():
            halo_from(k, side).wait_recv()
            middle = jnp.where(side == 0, centre_l, centre_r)
            share = halo[k, side, 0, 3:4, :]
            for p in range(pairs):
                z = scaled(halo[k, side, p], middle, near_rate)
                nST[p, 3 * side], nXS[p, 3 * side] = source_features(z, share)

        return act

    def rim_entries(j):
        side = side_of(j)
        entries = []
        for p in range(pairs):
            sums = ({}, {})
            for part in range(2):
                entries += block_items(
                    nST.at[p, 3 * side], nXS.at[p, 3 * side], nT.at[p, side, part], 0, "rim", sums[part], 1
                )
            entries.append(("then", near_add(p, side, sums)))
        return entries

    def springs(k):
        for copy in ring_copies(k):
            copy.wait_recv()
        upper = rows_of(atoms) < 4
        rolled = [pltpu.roll(X[k, p], 4, 0) for p in range(pairs)]
        before = [pltpu.roll(ring_p[k], 4, 0)] + rolled
        behind = rolled + [pltpu.roll(ring_n[k], 4, 0)]
        for p in range(pairs):
            bends = 2.0 * X[k, p] - rolled[p] - jnp.where(upper, before[p], behind[p + 1])
            AF[p] = -spring_rate * bends

    def kick(k, fast_step):
        for p in range(pairs):
            for t in range(2):
                lanes = slice(t * PA, (t + 1) * PA)
                z = scaled(X[k, p, :, lanes], centre, near_rate)
                coefficient = amp[:, lanes] * (near_scale / near_rate) * inverse[:, lanes]
                V[p, :, lanes] += fast_step * (AF[p, :, lanes] + coefficient * forces_of(z, nG[p, t]))

    def drift(k):
        for p in range(pairs):
            X[k + 1, p] = X[k, p] + time_step * V[p]

    def fast_phase(k):
        for copy in halo_copies(k) + ring_copies(k):
            copy.start()
        own_features(k)
        entries = own_entries(None) + [lambda: springs(k), rim_ready(k, 0)] + rim_entries(0)
        run_stream(entries + [rim_ready(k, 1)] + rim_entries(1))
        kick(k, time_step)
        drift(k)

    def slow_phase(e):
        k = INNER_STEPS * e
        for d in range(chips):
            pair_s[e, d] = partial_of(k, across(d, 1 - core))
        pair_copy(e).start()
        for d in range(chips):
            own_s[e, d] = partial_of(k, across(d, core))
        for copy in part_copies(e):
            copy.start()
        own_features(k)

        def send_joint():
            pair_copy(e).wait_recv()
            for d in range(chips):
                joint[e, d] = jnp.where(quarter == 3, charges, own_s[e, d] + pair_r[e, d])
            for copy in joint_copies(e) + halo_copies(k) + ring_copies(k):
                copy.start()

        def own_plane():
            total = joint[e, 0]
            for d in range(1, chips):
                for which in range(2):
                    part_copy(e, d, which).wait_recv()
                    total = total + part_r[e, d, which]
            Y[e] = total
            for t, half in enumerate(far_halves(total)):
                z = scaled(half, centre, far_rate)
                z = jnp.where(low_rows, z, 0.0)
                fST[2 + t], fXS[2 + t] = source_features(z, chg[:, t * PA:(t + 1) * PA])
                fT[t] = masked(target_features(z), 0)

        def send_far():
            halves = []
            for t, half in enumerate(far_halves(Y[e])):
                lanes = slice(t * PA, (t + 1) * PA)
                z = scaled(half, centre, far_rate)
                coefficient = chg[:, lanes] * (far_scale / far_rate)
                halves.append(coefficient * forces_of(z, fG[t]))
            far_s[e] = jnp.where(low_rows, halves[0], pltpu.roll(halves[1], 4, 0))
            for copy in far_copies(e):
                copy.start()

        sums = {}
        entries = own_entries(send_joint) + [own_plane]
        entries += far_items([(t, t, q, kind) for t, q, kind in far_own], sums)
        entries.append(("then", far_store({0: 0, 1: 1}, sums, True)))
        for j in range(2):
            side = side_of(j)

            def facing_plane(side=side):
                tile = None
                for d in range(chips):
                    joint_copy(e, side, d, left_s).wait_recv()
                    term = joint_r[e, side, d]
                    tile = term if tile is None else tile + term
                middle = jnp.where(side == 0, centre_l, centre_r)
                for t, half in enumerate(far_halves(tile)):
                    z = scaled(half, middle, far_rate)
                    z = jnp.where(low_rows, z, 0.0)
                    fST[4 * side + t], fXS[4 * side + t] = source_features(z, joint_r[e, side, 0, 4 * t + 3:4 * t + 4, :])

            entries.append(facing_plane)
            sums = {}
            facing = 1 + 3 * side
            entries += far_items([(0, 0, facing, "rim"), (1, 1, facing, "rim"), (2, side, 5 * side, "rim")], sums)
            entries.append(("then", far_store({0: 0, 1: 1, 2: side}, sums, False)))
            if j == 0:
                entries.append(rim_ready(k, 0))
        entries.append(("then", send_far))
        entries += rim_entries(0) + [lambda: springs(k), rim_ready(k, 1)] + rim_entries(1)

        run_stream(entries)

        edge = (e == 0) | (e == EVENTS - 1)
        kick(k, jnp.where(edge, 0.5 * time_step, time_step))
        slow_step = jnp.where(edge, 0.5 * INNER_STEPS * time_step, INNER_STEPS * time_step)
        for copy in far_copies(e):
            copy.wait_recv()
        ratio = float(beads_here)
        total = [[None, None] for _ in range(pairs)]
        for d in range(nb):
            tile = far_s[e] if d == 0 else far_r[e, d]
            c = lax.rem(me_b + nb - d, nb)
            turned = pltpu.roll(tile, 4, 0)
            doubled = (jnp.where(low_rows, tile, turned), jnp.where(low_rows, turned, tile))
            for p in range(pairs):
                first = table[c, first_bead + 2 * p] * ratio
                second = table[c, first_bead + 2 * p + 1] * ratio
                level = jnp.where(low_rows, first, second)
                for t in range(2):
                    term = level * doubled[t]
                    total[p][t] = term if d == 0 else total[p][t] + term
        for p in range(pairs):
            for t in range(2):
                lanes = slice(t * PA, (t + 1) * PA)
                V[p, :, lanes] += slow_step * inverse[:, lanes] * total[p][t]

    def outer(e, carry):
        slow_phase(e)

        @pl.when(e < OUTER_STEPS)
        def _():
            drift(INNER_STEPS * e)

            @pl.loop(1, INNER_STEPS)
            def _(i):
                fast_phase(INNER_STEPS * e + i)

        return carry

    lax.fori_loop(0, EVENTS, outer, 0)

    last = PHASES - 1
    for b in range(beads_here):
        p, r = b // 2, 4 * (b % 2)
        for c in range(3):
            moved[c, b:b + 1, :] = X[last, p, r + c:r + c + 1, :] - pos[c, b:b + 1, :]
            final[c, b:b + 1, :] = V[p, r + c:r + c + 1, :]

    @pl.loop(0, PHASES)
    def _(k):
        for copy in halo_copies(k) + ring_copies(k):
            copy.wait_send()

    @pl.loop(0, EVENTS)
    def _(e):
        for copy in [pair_copy(e)] + part_copies(e) + joint_copies(e) + far_copies(e):
            copy.wait_send()


def solution(mesh):
    nb, ns = mesh.shape["bead"], mesh.shape["slab"]

    def shards(positions, velocities, masses, amplitudes, charges):
        beads_here, _, atoms = positions.shape
        assert atoms == 2 * PA and beads_here % 2 == 0 and nb % 2 == 0 and ns > 2
        pairs = beads_here // 2
        table = jnp.asarray(contraction(beads_here * nb, nb))
        vmem = pl.BlockSpec(memory_space=pltpu.VMEM)
        out = jax.ShapeDtypeStruct((3, beads_here, atoms), F32)
        V, D = pltpu.VMEM, pltpu.SemaphoreType.DMA
        tile = (8, PA)

        def body(*refs):
            kernel(nb, ns, 2 * ns, *refs)

        shifted, speeds = pl.pallas_call(
            body,
            name="rod",
            out_shape=(pltpu.VMEM(out.shape, F32), pltpu.VMEM(out.shape, F32)),
            in_specs=[pl.BlockSpec(memory_space=pl.ANY)] * 6,
            out_specs=(vmem, vmem),
            scratch_shapes=[
                pltpu.SMEM(table.shape, F32), V(out.shape, F32), V(out.shape, F32),
                V((1, atoms), F32), V((1, atoms), F32), V((1, atoms), F32), D((6,)),
                V((PHASES, pairs, 8, atoms), F32),
                V((pairs, 8, atoms), F32),
                V((pairs, 8, atoms), F32),
                V((PHASES, 2, pairs) + tile, F32),
                V((PHASES, 8, atoms), F32), V((PHASES, 8, atoms), F32),
                V((EVENTS, nb // 2) + tile, F32), V((EVENTS, nb // 2) + tile, F32),
                V((EVENTS, nb // 2) + tile, F32), V((EVENTS, nb // 2, 2) + tile, F32),
                V((EVENTS, nb // 2) + tile, F32), V((EVENTS, 2, nb // 2) + tile, F32),
                V((EVENTS,) + tile, F32),
                V((EVENTS,) + tile, F32), V((EVENTS, nb) + tile, F32),
                V((pairs, 4, PA, FEATURES), BF16), V((pairs, 4, 16, PA), BF16),
                V((pairs, 2, 2, FEATURES, PA), BF16), V((pairs, 2) + tile, F32),
                V((6, PA, FEATURES), BF16), V((6, 16, PA), BF16),
                V((2, FEATURES, PA), BF16), V((2,) + tile, F32),
                D((PHASES, 2)), D((PHASES, 2)), D((PHASES, 2)), D((PHASES, 2)),
                D((EVENTS,)), D((EVENTS,)), D((EVENTS, nb // 2, 2)), D((EVENTS, nb // 2, 2)),
                D((EVENTS, 2, nb // 2)), D((EVENTS, 2, nb // 2)),
                D((EVENTS, nb)), D((EVENTS, nb)),
            ],
            compiler_params=pltpu.CompilerParams(collective_id=0, has_side_effects=True),
        )(table, positions.transpose(1, 0, 2), velocities.transpose(1, 0, 2), masses[None], amplitudes[None], charges[None])
        return shifted.transpose(1, 0, 2), speeds.transpose(1, 0, 2)

    both = P("bead", None, "slab")
    return jax.shard_map(
        shards, mesh=mesh, in_specs=(both, both, P("slab"), P("slab"), P("slab")), out_specs=(both, both), check_vma=False
    )
```

```python
import math

import jax
import jax.numpy as jnp
import numpy as np
from jax import lax
from jax.experimental import pallas as pl
from jax.experimental.pallas import tpu as pltpu
from jax.sharding import PartitionSpec as P

INNER_STEPS = 2
OUTER_STEPS = 2
PLANE_ATOMS = 512

time_step = 0.05
spring_rate = 25.0
near_scale = 4.0
far_scale = 2.0

MESH = pl.DeviceIdType.MESH
F32 = jnp.float32
BF16 = jnp.bfloat16
PA = PLANE_ATOMS
PHASES = INNER_STEPS * OUTER_STEPS + 1
EVENTS = OUTER_STEPS + 1
FEATURES = 64
HALF = PA // 2


def contraction(bead_count, small_count):
    bead_place = np.arange(bead_count, dtype=np.float64) / bead_count
    small_place = np.arange(small_count, dtype=np.float64) / small_count
    phase = 2.0 * np.pi * (bead_place[None, :] - small_place[:, None])
    modes = np.arange(1, small_count // 2, dtype=np.float64)
    total = 1.0 + np.cos(0.5 * small_count * phase)
    total = total + 2.0 * np.sum(np.cos(modes[:, None, None] * phase[None]), axis=0)
    return (total / bead_count).astype(np.float32)


def rows_of(width):
    return lax.broadcasted_iota(jnp.int32, (8, width), 0)


def cut(x):
    high = x.astype(BF16).astype(F32)
    rest = x - high
    mid = rest.astype(BF16).astype(F32)
    low = (rest - mid).astype(BF16).astype(F32)
    return high, mid, low


def scaled(x, first_centre, rate):
    quarter = rows_of(x.shape[1]) & 3
    centre = jnp.where(quarter == 0, first_centre, jnp.where(quarter == 3, 0.0, 1.0))
    return (x - centre) * rate


def source_features(z, share):
    quarter = rows_of(z.shape[1]) & 3
    square = 0.5 * z * z
    norm = pltpu.roll(square, 1, 0) + pltpu.roll(square, 2, 0) + pltpu.roll(square, 3, 0)
    high, mid, low = cut(jnp.where(quarter == 3, norm, z))
    one = jnp.ones_like(z)
    features = jnp.concatenate([high, high, mid, mid, high, low, one, jnp.zeros_like(z)], axis=0)
    weighted = share * jnp.where(quarter == 3, 1.0, z)
    first, second, _ = cut(weighted)
    return features.T.astype(BF16), jnp.concatenate([first, second], axis=0).astype(BF16)


def target_features(z):
    quarter = rows_of(z.shape[1]) & 3
    square = 0.5 * z * z
    norm = pltpu.roll(square, 1, 0) + pltpu.roll(square, 2, 0) + pltpu.roll(square, 3, 0)
    high, mid, low = cut(jnp.where(quarter == 3, norm, z))
    flat = quarter == 3
    own = jnp.where(
        flat,
        -high,
        jnp.where(quarter == 2, -pltpu.roll(mid, 7, 0), jnp.where(quarter == 1, -pltpu.roll(low, 6, 0), 0.0)),
    )
    high = jnp.where(flat, -1.0, high)
    mid = jnp.where(flat, 0.0, mid)
    low = jnp.where(flat, 0.0, low)
    return [high, mid, high, mid, low, high, own, jnp.zeros_like(z)]


def masked(groups, half):
    keep = (rows_of(groups[0].shape[1]) >> 2) == half
    return jnp.concatenate([jnp.where(keep, g, 0.0) for g in groups], axis=0).astype(BF16)


def weighted_sum(weighted, weight, pieces, flip):
    dims = (((1,), (1 if flip else 0,)), ((), ()))
    high = weight.astype(BF16)
    total = lax.dot_general(weighted, high, dims, preferred_element_type=F32)
    if pieces == 2:
        rest = (weight - high.astype(F32)).astype(BF16)
        total = total + lax.dot_general(weighted, rest, dims, preferred_element_type=F32)
    return total[:8] + total[8:]


def block_items(sources, weighted, targets, t, kind, sums, pieces, others=None):
    items = []
    for h in range(2):
        rows = slice(h * HALF, (h + 1) * HALF)
        width = HALF if kind == "self" and h == 0 else PA
        flips = None
        if kind == "self" and h == 1:
            flips = (weighted, HALF, (t, 1))
        if kind == "cross":
            flips = (others, PA, (1, h))
        items.append((sources, rows, weighted, targets, width, t, flips, sums, pieces))
    return items


def finish(item, exponent):
    _, rows, weighted, _, width, t, flips, sums, pieces = item
    weight = jnp.exp2(exponent)
    direct = weighted_sum(weighted[:, rows], weight, pieces, False)
    for half in range(width // HALF):
        part = direct[:, half * HALF:(half + 1) * HALF]
        sums[t, half] = sums[t, half] + part if (t, half) in sums else part
    if flips is not None:
        shares, depth, key = flips
        part = weighted_sum(shares[:, :depth], weight[:, :depth], pieces, True)
        sums[key] = sums[key] + part if key in sums else part


def run_stream(entries):
    waiting, pending = None, []
    for entry in entries:
        if not isinstance(entry, tuple):
            entry()
            continue
        if entry[0] == "then":
            pending.append(entry[1])
            continue
        sources, rows, _, targets, width = entry[:5]
        exponent = jnp.dot(sources[rows, :], targets[:, :width], preferred_element_type=F32)
        if waiting is not None:
            finish(*waiting)
        for act in pending:
            act()
        waiting, pending = (entry, exponent), []
    finish(*waiting)
    for act in pending:
        act()


def forces_of(z, sums):
    quarter = rows_of(z.shape[1]) & 3
    plain = jnp.where(quarter == 3, sums, 0.0)
    spread = pltpu.roll(plain, 7, 0) + pltpu.roll(plain, 6, 0) + pltpu.roll(plain, 5, 0)
    return jnp.where(quarter == 3, 0.0, z * spread - sums)


def kernel(
    nb, ns, planes_total,
    table_h, pos_h, vel_h, mass_h, amp_h, chg_h,
    result,
    table, pos, vel, mass, amp, chg, in_sem,
    X, V, AF, halo, ring_p, ring_n,
    part_s, part_r, Y, far_s, far_r,
    nST, nXS, nT, nG, fST, fXS, fT, fG,
    halo_ss, halo_rs, ring_ss, ring_rs, part_ss, part_rs, far_ss, far_rs,
):
    me_b = lax.axis_index("bead")
    me_s = lax.axis_index("slab")
    left_s = lax.rem(me_s + ns - 1, ns)
    right_s = lax.rem(me_s + 1, ns)
    left = (me_b, left_s)
    right = (me_b, right_s)
    prev = (lax.rem(me_b + nb - 1, nb), me_s)
    after = (lax.rem(me_b + 1, nb), me_s)
    pairs = X.shape[1]
    beads_here = 2 * pairs
    atoms = X.shape[3]
    first_bead = me_b * beads_here

    def peer(d):
        return lax.rem(me_b + d, nb)

    def remote(src, dst, ss, rs, to):
        return pltpu.make_async_remote_copy(
            src_ref=src, dst_ref=dst, send_sem=ss, recv_sem=rs, device_id=to, device_id_type=MESH
        )

    barrier = pltpu.get_barrier_semaphore()
    for d in range(nb):
        for side in (left_s, right_s):
            pl.semaphore_signal(barrier, inc=1, device_id=(peer(d), side), device_id_type=MESH)
    for d in range(1, nb):
        other = (lax.rem(me_b + d, nb), me_s)
        pl.semaphore_signal(barrier, inc=1, device_id=other, device_id_type=MESH)

    loads = [
        pltpu.make_async_copy(src, dst, in_sem.at[i])
        for i, (src, dst) in enumerate(
            ((pos_h, pos), (vel_h, vel), (amp_h, amp), (chg_h, chg), (mass_h, mass), (table_h, table))
        )
    ]
    for load in loads:
        load.start()
    X[0] = jnp.zeros((pairs, 8, atoms), F32)
    V[...] = jnp.zeros_like(V)
    for load in loads:
        load.wait()
    for b in range(beads_here):
        p, r = b // 2, 4 * (b % 2)
        for c in range(3):
            X[0, p, r + c:r + c + 1, :] = pos[c, b:b + 1, :]
            V[p, r + c:r + c + 1, :] = vel[c, b:b + 1, :]
    for p in range(pairs):
        for r in (3, 7):
            X[0, p, r:r + 1, :] = amp[...]
    quarter = rows_of(PA) & 3
    charges = jnp.where(rows_of(PA) < 4, chg[:, :PA], chg[:, PA:])

    centre = (me_s * 2).astype(F32) + 1.0
    span = float(planes_total)
    centre_l = centre + jnp.where(me_s == 0, span, 0.0)
    centre_r = centre - jnp.where(me_s == ns - 1, span, 0.0)
    near_rate = math.sqrt(near_scale / math.log(2.0))
    far_rate = math.sqrt(far_scale / math.log(2.0))

    inverse = 1.0 / mass[...]

    pl.semaphore_wait(barrier, 3 * nb - 1)

    def halo_copies(k):
        return [
            remote(X.at[k, :, :, pl.ds(0, PA)], halo.at[k, 1], halo_ss.at[k, 1], halo_rs.at[k, 1], left),
            remote(X.at[k, :, :, pl.ds(atoms - PA, PA)], halo.at[k, 0], halo_ss.at[k, 0], halo_rs.at[k, 0], right),
        ]

    def halo_from(k, side):
        return remote(X.at[k, :, :, pl.ds(0, PA)], halo.at[k, side], halo_ss.at[k, side], halo_rs.at[k, side], left)

    def ring_copies(k):
        return [
            remote(X.at[k, pairs - 1], ring_p.at[k], ring_ss.at[k, 0], ring_rs.at[k, 0], after),
            remote(X.at[k, 0], ring_n.at[k], ring_ss.at[k, 1], ring_rs.at[k, 1], prev),
        ]

    def far_copies(e):
        return [
            remote(far_s.at[e], far_r.at[e, d], far_ss.at[e, d], far_rs.at[e, d], (lax.rem(me_b + d, nb), me_s))
            for d in range(1, nb)
        ]

    def part_copy(e, place, d, to):
        return remote(
            part_s.at[e, d], part_r.at[e, place, d], part_ss.at[e, place, d], part_rs.at[e, place, d], (peer(d), to)
        )

    def parts_to(e, d):
        sides = [part_copy(e, 1, d, left_s), part_copy(e, 0, d, right_s)]
        return sides + ([part_copy(e, 2, d, me_s)] if d else [])

    def part_copies(e):
        return [copy for d in range(nb) for copy in parts_to(e, d)]

    low_rows = rows_of(PA) < 4

    def partial_of(k, c):
        total = None
        for p in range(pairs):
            first = table[c, first_bead + 2 * p]
            second = table[c, first_bead + 2 * p + 1]
            term = jnp.where(rows_of(atoms) < 4, first, second) * X[k, p]
            total = term if total is None else total + term
        total = total + pltpu.roll(total, 4, 0)
        return jnp.where(low_rows, total[:, :PA], total[:, PA:])

    def far_halves(tile):
        first = jnp.where(low_rows, tile, 0.0)
        second = jnp.where(low_rows, pltpu.roll(tile, 4, 0), 0.0)
        return first, second

    def side_of(j):
        return jnp.where(me_s == 0, 1 - j, j)

    near_own = ((0, 1, "self"), (0, 2, "cross"), (1, 2, "self"))
    far_own = ((0, 2, "self"), (0, 3, "cross"), (1, 3, "self"))

    def near_own_items(p, part, sums):
        items = []
        for t, q, kind in near_own:
            others = nXS.at[p, 1] if kind == "cross" else None
            items += block_items(nST.at[p, q], nXS.at[p, q], nT.at[p, t, part], t, kind, sums, 1, others)
        return items

    def far_items(blocks, sums):
        items = []
        for label, t, q, kind in blocks:
            others = fXS.at[2] if kind == "cross" else None
            items += block_items(fST.at[q], fXS.at[q], fT.at[t], label, kind, sums, 2, others)
        return items

    def near_store(p, sums):
        def act():
            for t, half in sums[0]:
                lanes = slice(half * HALF, (half + 1) * HALF)
                nG[p, t, :, lanes] = jnp.where(rows_of(HALF) < 4, sums[0][t, half], sums[1][t, half])
        return act

    def near_add(p, side, sums):
        def act():
            for half in range(2):
                lanes = slice(half * HALF, (half + 1) * HALF)
                nG[p, side, :, lanes] += jnp.where(rows_of(HALF) < 4, sums[0][0, half], sums[1][0, half])
        return act

    def far_store(places, sums, first):
        def act():
            for label, half in sorted(sums):
                lanes = slice(half * HALF, (half + 1) * HALF)
                if first:
                    fG[places[label], :, lanes] = sums[label, half]
                else:
                    fG[places[label], :, lanes] += sums[label, half]
        return act

    def own_features(k):
        for p in range(pairs):
            for t in range(2):
                lanes = slice(t * PA, (t + 1) * PA)
                z = scaled(X[k, p, :, lanes], centre, near_rate)
                nST[p, 1 + t], nXS[p, 1 + t] = source_features(z, amp[:, lanes])
                groups = target_features(z)
                nT[p, t, 0] = masked(groups, 0)
                nT[p, t, 1] = masked(groups, 1)

    def own_entries(after_first=None):
        entries = []
        for p in range(pairs):
            sums = ({}, {})
            for part in range(2):
                entries += near_own_items(p, part, sums[part])
                if p == 0 and part == 0 and after_first is not None:
                    entries.append(after_first)
            entries.append(("then", near_store(p, sums)))
        return entries

    def rim_ready(k, j):
        side = side_of(j)

        def act():
            halo_from(k, side).wait_recv()
            middle = jnp.where(side == 0, centre_l, centre_r)
            share = halo[k, side, 0, 3:4, :]
            for p in range(pairs):
                z = scaled(halo[k, side, p], middle, near_rate)
                nST[p, 3 * side], nXS[p, 3 * side] = source_features(z, share)

        return act

    def rim_entries(j):
        side = side_of(j)
        entries = []
        for p in range(pairs):
            sums = ({}, {})
            for part in range(2):
                entries += block_items(
                    nST.at[p, 3 * side], nXS.at[p, 3 * side], nT.at[p, side, part], 0, "rim", sums[part], 1
                )
            entries.append(("then", near_add(p, side, sums)))
        return entries

    def springs(k):
        for copy in ring_copies(k):
            copy.wait_recv()
        upper = rows_of(atoms) < 4
        rolled = [pltpu.roll(X[k, p], 4, 0) for p in range(pairs)]
        before = [pltpu.roll(ring_p[k], 4, 0)] + rolled
        behind = rolled + [pltpu.roll(ring_n[k], 4, 0)]
        for p in range(pairs):
            bends = 2.0 * X[k, p] - rolled[p] - jnp.where(upper, before[p], behind[p + 1])
            AF[p] = -spring_rate * bends

    def kick(k, fast_step):
        for p in range(pairs):
            for t in range(2):
                lanes = slice(t * PA, (t + 1) * PA)
                z = scaled(X[k, p, :, lanes], centre, near_rate)
                coefficient = amp[:, lanes] * (near_scale / near_rate) * inverse[:, lanes]
                V[p, :, lanes] += fast_step * (AF[p, :, lanes] + coefficient * forces_of(z, nG[p, t]))

    def drift(k):
        for p in range(pairs):
            X[k + 1, p] = X[k, p] + time_step * V[p]

    def fast_phase(k):
        for copy in halo_copies(k) + ring_copies(k):
            copy.start()
        own_features(k)
        entries = own_entries() + [lambda: springs(k), rim_ready(k, 0)] + rim_entries(0)
        run_stream(entries + [rim_ready(k, 1)] + rim_entries(1))
        kick(k, time_step)
        drift(k)

    def slow_phase(e):
        k = INNER_STEPS * e
        for d in range(nb):
            part_s[e, d] = jnp.where(quarter == 3, charges, partial_of(k, peer(d)))
            for copy in parts_to(e, d):
                copy.start()
        own_features(k)

        def send_edges():
            for copy in halo_copies(k) + ring_copies(k):
                copy.start()

        def own_plane():
            total = part_s[e, 0]
            for d in range(1, nb):
                part_copy(e, 2, d, me_s).wait_recv()
                total = total + part_r[e, 2, d]
            Y[e] = total
            for t, half in enumerate(far_halves(total)):
                z = scaled(half, centre, far_rate)
                z = jnp.where(low_rows, z, 0.0)
                fST[2 + t], fXS[2 + t] = source_features(z, chg[:, t * PA:(t + 1) * PA])
                fT[t] = masked(target_features(z), 0)

        def send_far():
            halves = []
            for t, half in enumerate(far_halves(Y[e])):
                lanes = slice(t * PA, (t + 1) * PA)
                z = scaled(half, centre, far_rate)
                coefficient = chg[:, lanes] * (far_scale / far_rate)
                halves.append(coefficient * forces_of(z, fG[t]))
            far_s[e] = jnp.where(low_rows, halves[0], pltpu.roll(halves[1], 4, 0))
            for copy in far_copies(e):
                copy.start()

        sums = {}
        entries = own_entries(send_edges) + [own_plane]
        entries += far_items([(t, t, q, kind) for t, q, kind in far_own], sums)
        entries.append(("then", far_store({0: 0, 1: 1}, sums, True)))
        for j in range(2):
            side = side_of(j)

            def facing_plane(side=side):
                tile = None
                for d in range(nb):
                    part_copy(e, side, d, left_s).wait_recv()
                    term = part_r[e, side, d]
                    tile = term if tile is None else tile + term
                middle = jnp.where(side == 0, centre_l, centre_r)
                for t, half in enumerate(far_halves(tile)):
                    z = scaled(half, middle, far_rate)
                    z = jnp.where(low_rows, z, 0.0)
                    fST[4 * side + t], fXS[4 * side + t] = source_features(z, part_r[e, side, 0, 4 * t + 3:4 * t + 4, :])

            entries.append(facing_plane)
            sums = {}
            facing = 1 + 3 * side
            entries += far_items([(0, 0, facing, "rim"), (1, 1, facing, "rim"), (2, side, 5 * side, "rim")], sums)
            entries.append(("then", far_store({0: 0, 1: 1, 2: side}, sums, False)))
            if j == 0:
                entries.append(rim_ready(k, 0))
        entries.append(("then", send_far))
        entries += rim_entries(0) + [lambda: springs(k), rim_ready(k, 1)] + rim_entries(1)

        run_stream(entries)

        edge = (e == 0) | (e == EVENTS - 1)
        kick(k, jnp.where(edge, 0.5 * time_step, time_step))
        slow_step = jnp.where(edge, 0.5 * INNER_STEPS * time_step, INNER_STEPS * time_step)
        for copy in far_copies(e):
            copy.wait_recv()
        ratio = float(beads_here)
        total = [[None, None] for _ in range(pairs)]
        for d in range(nb):
            tile = far_s[e] if d == 0 else far_r[e, d]
            c = lax.rem(me_b + nb - d, nb)
            turned = pltpu.roll(tile, 4, 0)
            doubled = (jnp.where(low_rows, tile, turned), jnp.where(low_rows, turned, tile))
            for p in range(pairs):
                first = table[c, first_bead + 2 * p] * ratio
                second = table[c, first_bead + 2 * p + 1] * ratio
                level = jnp.where(low_rows, first, second)
                for t in range(2):
                    term = level * doubled[t]
                    total[p][t] = term if d == 0 else total[p][t] + term
        for p in range(pairs):
            for t in range(2):
                lanes = slice(t * PA, (t + 1) * PA)
                V[p, :, lanes] += slow_step * inverse[:, lanes] * total[p][t]

    def outer(e, carry):
        slow_phase(e)

        @pl.when(e < OUTER_STEPS)
        def _():
            drift(INNER_STEPS * e)

            @pl.loop(1, INNER_STEPS)
            def _(i):
                fast_phase(INNER_STEPS * e + i)

        return carry

    lax.fori_loop(0, EVENTS, outer, 0)

    last = PHASES - 1
    for b in range(beads_here):
        p, r = b // 2, 4 * (b % 2)
        for c in range(3):
            result[c, b:b + 1, :] = X[last, p, r + c:r + c + 1, :] - pos[c, b:b + 1, :]
            result[3 + c, b:b + 1, :] = V[p, r + c:r + c + 1, :]

    @pl.loop(0, PHASES)
    def _(k):
        for copy in halo_copies(k) + ring_copies(k):
            copy.wait_send()

    @pl.loop(0, EVENTS)
    def _(e):
        for copy in part_copies(e) + far_copies(e):
            copy.wait_send()


def solution(mesh):
    nb, ns = mesh.shape["bead"], mesh.shape["slab"]

    def shards(positions, velocities, masses, amplitudes, charges):
        beads_here, _, atoms = positions.shape
        assert atoms == 2 * PA and beads_here % 2 == 0 and ns > 2
        pairs = beads_here // 2
        table = jnp.asarray(contraction(beads_here * nb, nb))
        vmem = pl.BlockSpec(memory_space=pltpu.VMEM)
        out = jax.ShapeDtypeStruct((3, beads_here, atoms), F32)
        V, D = pltpu.VMEM, pltpu.SemaphoreType.DMA
        tile = (8, PA)

        def body(*refs):
            kernel(nb, ns, 2 * ns, *refs)

        result = pl.pallas_call(
            body,
            name="rod",
            out_shape=pltpu.VMEM((6,) + out.shape[1:], F32),
            in_specs=[pl.BlockSpec(memory_space=pl.ANY)] * 6,
            out_specs=vmem,
            scratch_shapes=[
                pltpu.SMEM(table.shape, F32), V(out.shape, F32), V(out.shape, F32),
                V((1, atoms), F32), V((1, atoms), F32), V((1, atoms), F32), D((6,)),
                V((PHASES, pairs, 8, atoms), F32),
                V((pairs, 8, atoms), F32),
                V((pairs, 8, atoms), F32),
                V((PHASES, 2, pairs) + tile, F32),
                V((PHASES, 8, atoms), F32), V((PHASES, 8, atoms), F32),
                V((EVENTS, nb) + tile, F32), V((EVENTS, 3, nb) + tile, F32),
                V((EVENTS,) + tile, F32),
                V((EVENTS,) + tile, F32), V((EVENTS, nb) + tile, F32),
                V((pairs, 4, PA, FEATURES), BF16), V((pairs, 4, 16, PA), BF16),
                V((pairs, 2, 2, FEATURES, PA), BF16), V((pairs, 2) + tile, F32),
                V((6, PA, FEATURES), BF16), V((6, 16, PA), BF16),
                V((2, FEATURES, PA), BF16), V((2,) + tile, F32),
                D((PHASES, 2)), D((PHASES, 2)), D((PHASES, 2)), D((PHASES, 2)),
                D((EVENTS, 3, nb)), D((EVENTS, 3, nb)),
                D((EVENTS, nb)), D((EVENTS, nb)),
            ],
            compiler_params=pltpu.CompilerParams(collective_id=0, has_side_effects=True),
        )(table, positions.transpose(1, 0, 2), velocities.transpose(1, 0, 2), masses[None], amplitudes[None], charges[None])
        return result[:3].transpose(1, 0, 2), result[3:].transpose(1, 0, 2)

    both = P("bead", None, "slab")
    return jax.shard_map(
        shards, mesh=mesh, in_specs=(both, both, P("slab"), P("slab"), P("slab")), out_specs=(both, both), check_vma=False
    )
```

```python
import math

import jax
import jax.numpy as jnp
import numpy as np
from jax import lax
from jax.experimental import pallas as pl
from jax.experimental.pallas import tpu as pltpu
from jax.sharding import PartitionSpec as P

INNER_STEPS = 2
OUTER_STEPS = 2
PLANE_ATOMS = 512

time_step = 0.05
spring_rate = 25.0
near_scale = 4.0
far_scale = 2.0

MESH = pl.DeviceIdType.MESH
F32 = jnp.float32
BF16 = jnp.bfloat16
PA = PLANE_ATOMS
PHASES = INNER_STEPS * OUTER_STEPS + 1
EVENTS = OUTER_STEPS + 1
FEATURES = 64
HALF = PA // 2


def contraction(bead_count, small_count):
    bead_place = np.arange(bead_count, dtype=np.float64) / bead_count
    small_place = np.arange(small_count, dtype=np.float64) / small_count
    phase = 2.0 * np.pi * (bead_place[None, :] - small_place[:, None])
    modes = np.arange(1, small_count // 2, dtype=np.float64)
    total = 1.0 + np.cos(0.5 * small_count * phase)
    total = total + 2.0 * np.sum(np.cos(modes[:, None, None] * phase[None]), axis=0)
    return (total / bead_count).astype(np.float32)


def rows_of(width):
    return lax.broadcasted_iota(jnp.int32, (8, width), 0)


def cut(x):
    high = x.astype(BF16).astype(F32)
    rest = x - high
    mid = rest.astype(BF16).astype(F32)
    low = (rest - mid).astype(BF16).astype(F32)
    return high, mid, low


def scaled(x, first_centre, rate):
    quarter = rows_of(x.shape[1]) & 3
    centre = jnp.where(quarter == 0, first_centre, jnp.where(quarter == 3, 0.0, 1.0))
    return (x - centre) * rate


def source_features(z, share):
    quarter = rows_of(z.shape[1]) & 3
    square = 0.5 * z * z
    norm = pltpu.roll(square, 1, 0) + pltpu.roll(square, 2, 0) + pltpu.roll(square, 3, 0)
    high, mid, low = cut(jnp.where(quarter == 3, norm, z))
    one = jnp.ones_like(z)
    features = jnp.concatenate([high, high, mid, mid, high, low, one, jnp.zeros_like(z)], axis=0)
    weighted = share * jnp.where(quarter == 3, 1.0, z)
    first, second, _ = cut(weighted)
    return features.T.astype(BF16), jnp.concatenate([first, second], axis=0).astype(BF16)


def target_features(z):
    quarter = rows_of(z.shape[1]) & 3
    square = 0.5 * z * z
    norm = pltpu.roll(square, 1, 0) + pltpu.roll(square, 2, 0) + pltpu.roll(square, 3, 0)
    high, mid, low = cut(jnp.where(quarter == 3, norm, z))
    flat = quarter == 3
    own = jnp.where(
        flat,
        -high,
        jnp.where(quarter == 2, -pltpu.roll(mid, 7, 0), jnp.where(quarter == 1, -pltpu.roll(low, 6, 0), 0.0)),
    )
    high = jnp.where(flat, -1.0, high)
    mid = jnp.where(flat, 0.0, mid)
    low = jnp.where(flat, 0.0, low)
    return [high, mid, high, mid, low, high, own, jnp.zeros_like(z)]


def masked(groups, half):
    keep = (rows_of(groups[0].shape[1]) >> 2) == half
    return jnp.concatenate([jnp.where(keep, g, 0.0) for g in groups], axis=0).astype(BF16)


def weighted_sum(weighted, weight, pieces, flip):
    dims = (((1,), (1 if flip else 0,)), ((), ()))
    high = weight.astype(BF16)
    total = lax.dot_general(weighted, high, dims, preferred_element_type=F32)
    if pieces == 2:
        rest = (weight - high.astype(F32)).astype(BF16)
        total = total + lax.dot_general(weighted, rest, dims, preferred_element_type=F32)
    return total[:8] + total[8:]


def block_items(sources, weighted, targets, t, kind, sums, pieces, others=None):
    items = []
    for h in range(2):
        rows = slice(h * HALF, (h + 1) * HALF)
        width = HALF if kind == "self" and h == 0 else PA
        flips = None
        if kind == "self" and h == 1:
            flips = (weighted, HALF, (t, 1))
        if kind == "cross":
            flips = (others, PA, (1, h))
        items.append((sources, rows, weighted, targets, width, t, flips, sums, pieces))
    return items


def finish(item, exponent):
    _, rows, weighted, _, width, t, flips, sums, pieces = item
    weight = jnp.exp2(exponent)
    direct = weighted_sum(weighted[:, rows], weight, pieces, False)
    for half in range(width // HALF):
        part = direct[:, half * HALF:(half + 1) * HALF]
        sums[t, half] = sums[t, half] + part if (t, half) in sums else part
    if flips is not None:
        shares, depth, key = flips
        part = weighted_sum(shares[:, :depth], weight[:, :depth], pieces, True)
        sums[key] = sums[key] + part if key in sums else part


def run_stream(entries):
    waiting, pending = None, []
    for entry in entries:
        if not isinstance(entry, tuple):
            entry()
            continue
        if entry[0] == "then":
            pending.append(entry[1])
            continue
        sources, rows, _, targets, width = entry[:5]
        exponent = jnp.dot(sources[rows, :], targets[:, :width], preferred_element_type=F32)
        if waiting is not None:
            finish(*waiting)
        for act in pending:
            act()
        waiting, pending = (entry, exponent), []
    finish(*waiting)
    for act in pending:
        act()


def forces_of(z, sums):
    quarter = rows_of(z.shape[1]) & 3
    plain = jnp.where(quarter == 3, sums, 0.0)
    spread = pltpu.roll(plain, 7, 0) + pltpu.roll(plain, 6, 0) + pltpu.roll(plain, 5, 0)
    return jnp.where(quarter == 3, 0.0, z * spread - sums)


def kernel(
    nb, ns, planes_total,
    table_h, pos_h, vel_h, mass_h, amp_h, chg_h,
    result,
    table, pos, vel, mass, amp, chg, in_sem,
    X, V, AF, halo, ring_p, ring_n,
    part_s, part_r, Y, far_s, far_r,
    nST, nXS, nT, nG, fST, fXS, fT, fG,
    halo_ss, halo_rs, ring_ss, ring_rs, part_ss, part_rs, far_ss, far_rs,
):
    me_b = lax.axis_index("bead")
    me_s = lax.axis_index("slab")
    left_s = lax.rem(me_s + ns - 1, ns)
    right_s = lax.rem(me_s + 1, ns)
    left = (me_b, left_s)
    right = (me_b, right_s)
    prev = (lax.rem(me_b + nb - 1, nb), me_s)
    after = (lax.rem(me_b + 1, nb), me_s)
    pairs = X.shape[1]
    beads_here = 2 * pairs
    atoms = X.shape[3]
    first_bead = me_b * beads_here

    def peer(d):
        return lax.rem(me_b + d, nb)

    def remote(src, dst, ss, rs, to):
        return pltpu.make_async_remote_copy(
            src_ref=src, dst_ref=dst, send_sem=ss, recv_sem=rs, device_id=to, device_id_type=MESH
        )

    barrier = pltpu.get_barrier_semaphore()
    for d in range(nb):
        for side in (left_s, right_s):
            pl.semaphore_signal(barrier, inc=1, device_id=(peer(d), side), device_id_type=MESH)
    for d in range(1, nb):
        other = (lax.rem(me_b + d, nb), me_s)
        pl.semaphore_signal(barrier, inc=1, device_id=other, device_id_type=MESH)

    loads = [
        pltpu.make_async_copy(src, dst, in_sem.at[i])
        for i, (src, dst) in enumerate(
            ((pos_h, pos), (vel_h, vel), (amp_h, amp), (chg_h, chg), (mass_h, mass), (table_h, table))
        )
    ]
    for load in loads:
        load.start()
    X[0] = jnp.zeros((pairs, 8, atoms), F32)
    V[...] = jnp.zeros_like(V)
    for load in loads:
        load.wait()
    for b in range(beads_here):
        p, r = b // 2, 4 * (b % 2)
        for c in range(3):
            X[0, p, r + c:r + c + 1, :] = pos[c, b:b + 1, :]
            V[p, r + c:r + c + 1, :] = vel[c, b:b + 1, :]
    for p in range(pairs):
        for r in (3, 7):
            X[0, p, r:r + 1, :] = amp[...]
    quarter = rows_of(PA) & 3
    charges = jnp.where(rows_of(PA) < 4, chg[:, :PA], chg[:, PA:])

    centre = (me_s * 2).astype(F32) + 1.0
    span = float(planes_total)
    centre_l = centre + jnp.where(me_s == 0, span, 0.0)
    centre_r = centre - jnp.where(me_s == ns - 1, span, 0.0)
    near_rate = math.sqrt(near_scale / math.log(2.0))
    far_rate = math.sqrt(far_scale / math.log(2.0))

    inverse = 1.0 / mass[...]

    pl.semaphore_wait(barrier, 3 * nb - 1)

    def halo_copies(k):
        return [
            remote(X.at[k, :, :, pl.ds(0, PA)], halo.at[k, 1], halo_ss.at[k, 1], halo_rs.at[k, 1], left),
            remote(X.at[k, :, :, pl.ds(atoms - PA, PA)], halo.at[k, 0], halo_ss.at[k, 0], halo_rs.at[k, 0], right),
        ]

    def halo_from(k, side):
        return remote(X.at[k, :, :, pl.ds(0, PA)], halo.at[k, side], halo_ss.at[k, side], halo_rs.at[k, side], left)

    def ring_copies(k):
        return [
            remote(X.at[k, pairs - 1], ring_p.at[k], ring_ss.at[k, 0], ring_rs.at[k, 0], after),
            remote(X.at[k, 0], ring_n.at[k], ring_ss.at[k, 1], ring_rs.at[k, 1], prev),
        ]

    def far_copies(e):
        return [
            remote(far_s.at[e], far_r.at[e, d], far_ss.at[e, d], far_rs.at[e, d], (lax.rem(me_b + d, nb), me_s))
            for d in range(1, nb)
        ]

    def part_copy(e, place, d, to):
        return remote(
            part_s.at[e, d], part_r.at[e, place, d], part_ss.at[e, place, d], part_rs.at[e, place, d], (peer(d), to)
        )

    def parts_to(e, d):
        sides = [part_copy(e, 1, d, left_s), part_copy(e, 0, d, right_s)]
        return sides + ([part_copy(e, 2, d, me_s)] if d else [])

    def part_copies(e):
        return [copy for d in range(nb) for copy in parts_to(e, d)]

    low_rows = rows_of(PA) < 4

    def partial_of(k, c):
        total = None
        for p in range(pairs):
            first = table[c, first_bead + 2 * p]
            second = table[c, first_bead + 2 * p + 1]
            term = jnp.where(rows_of(atoms) < 4, first, second) * X[k, p]
            total = term if total is None else total + term
        total = total + pltpu.roll(total, 4, 0)
        return jnp.where(low_rows, total[:, :PA], total[:, PA:])

    def far_halves(tile):
        first = jnp.where(low_rows, tile, 0.0)
        second = jnp.where(low_rows, pltpu.roll(tile, 4, 0), 0.0)
        return first, second

    def side_of(j):
        return jnp.where(lax.rem(me_s, 2) == 0, 1 - j, j)

    near_own = ((0, 1, "self"), (0, 2, "cross"), (1, 2, "self"))
    far_own = ((0, 2, "self"), (0, 3, "cross"), (1, 3, "self"))

    def near_own_items(p, part, sums):
        items = []
        for t, q, kind in near_own:
            others = nXS.at[p, 1] if kind == "cross" else None
            items += block_items(nST.at[p, q], nXS.at[p, q], nT.at[p, t, part], t, kind, sums, 1, others)
        return items

    def far_items(blocks, sums):
        items = []
        for label, t, q, kind in blocks:
            others = fXS.at[2] if kind == "cross" else None
            items += block_items(fST.at[q], fXS.at[q], fT.at[t], label, kind, sums, 2, others)
        return items

    def near_store(p, sums):
        def act():
            for t, half in sums[0]:
                lanes = slice(half * HALF, (half + 1) * HALF)
                nG[p, t, :, lanes] = jnp.where(rows_of(HALF) < 4, sums[0][t, half], sums[1][t, half])
        return act

    def near_add(p, side, sums):
        def act():
            for half in range(2):
                lanes = slice(half * HALF, (half + 1) * HALF)
                nG[p, side, :, lanes] += jnp.where(rows_of(HALF) < 4, sums[0][0, half], sums[1][0, half])
        return act

    def far_store(places, sums, first):
        def act():
            for label, half in sorted(sums):
                lanes = slice(half * HALF, (half + 1) * HALF)
                if first:
                    fG[places[label], :, lanes] = sums[label, half]
                else:
                    fG[places[label], :, lanes] += sums[label, half]
        return act

    def own_features(k):
        for p in range(pairs):
            for t in range(2):
                lanes = slice(t * PA, (t + 1) * PA)
                z = scaled(X[k, p, :, lanes], centre, near_rate)
                nST[p, 1 + t], nXS[p, 1 + t] = source_features(z, amp[:, lanes])
                groups = target_features(z)
                nT[p, t, 0] = masked(groups, 0)
                nT[p, t, 1] = masked(groups, 1)

    def own_entries(after_first=None):
        entries = []
        for p in range(pairs):
            sums = ({}, {})
            for part in range(2):
                entries += near_own_items(p, part, sums[part])
                if p == 0 and part == 0 and after_first is not None:
                    entries.append(after_first)
            entries.append(("then", near_store(p, sums)))
        return entries

    def rim_ready(k, j):
        side = side_of(j)

        def act():
            halo_from(k, side).wait_recv()
            middle = jnp.where(side == 0, centre_l, centre_r)
            share = halo[k, side, 0, 3:4, :]
            for p in range(pairs):
                z = scaled(halo[k, side, p], middle, near_rate)
                nST[p, 3 * side], nXS[p, 3 * side] = source_features(z, share)

        return act

    def rim_entries(j):
        side = side_of(j)
        entries = []
        for p in range(pairs):
            sums = ({}, {})
            for part in range(2):
                entries += block_items(
                    nST.at[p, 3 * side], nXS.at[p, 3 * side], nT.at[p, side, part], 0, "rim", sums[part], 1
                )
            entries.append(("then", near_add(p, side, sums)))
        return entries

    def springs(k):
        for copy in ring_copies(k):
            copy.wait_recv()
        upper = rows_of(atoms) < 4
        rolled = [pltpu.roll(X[k, p], 4, 0) for p in range(pairs)]
        before = [pltpu.roll(ring_p[k], 4, 0)] + rolled
        behind = rolled + [pltpu.roll(ring_n[k], 4, 0)]
        for p in range(pairs):
            bends = 2.0 * X[k, p] - rolled[p] - jnp.where(upper, before[p], behind[p + 1])
            AF[p] = -spring_rate * bends

    def kick(k, fast_step):
        for p in range(pairs):
            for t in range(2):
                lanes = slice(t * PA, (t + 1) * PA)
                z = scaled(X[k, p, :, lanes], centre, near_rate)
                coefficient = amp[:, lanes] * (near_scale / near_rate) * inverse[:, lanes]
                V[p, :, lanes] += fast_step * (AF[p, :, lanes] + coefficient * forces_of(z, nG[p, t]))

    def drift(k):
        for p in range(pairs):
            X[k + 1, p] = X[k, p] + time_step * V[p]

    def fast_phase(k):
        for copy in halo_copies(k) + ring_copies(k):
            copy.start()
        own_features(k)
        entries = own_entries() + [lambda: springs(k), rim_ready(k, 0)] + rim_entries(0)
        run_stream(entries + [rim_ready(k, 1)] + rim_entries(1))
        for copy in halo_copies(k) + ring_copies(k):
            copy.wait_send()
        kick(k, time_step)
        drift(k)

    def slow_phase(e):
        k = INNER_STEPS * e
        for d in range(nb):
            part_s[e, d] = jnp.where(quarter == 3, charges, partial_of(k, peer(d)))
            for copy in parts_to(e, d):
                copy.start()
        own_features(k)

        def send_edges():
            for copy in halo_copies(k) + ring_copies(k):
                copy.start()

        def own_plane():
            total = part_s[e, 0]
            for d in range(1, nb):
                part_copy(e, 2, d, me_s).wait_recv()
                total = total + part_r[e, 2, d]
            Y[e] = total
            for t, half in enumerate(far_halves(total)):
                z = scaled(half, centre, far_rate)
                z = jnp.where(low_rows, z, 0.0)
                fST[2 + t], fXS[2 + t] = source_features(z, chg[:, t * PA:(t + 1) * PA])
                fT[t] = masked(target_features(z), 0)

        def send_far():
            halves = []
            for t, half in enumerate(far_halves(Y[e])):
                lanes = slice(t * PA, (t + 1) * PA)
                z = scaled(half, centre, far_rate)
                coefficient = chg[:, lanes] * (far_scale / far_rate)
                halves.append(coefficient * forces_of(z, fG[t]))
            far_s[e] = jnp.where(low_rows, halves[0], pltpu.roll(halves[1], 4, 0))
            for copy in far_copies(e):
                copy.start()

        sums = {}
        entries = own_entries(send_edges) + [own_plane]
        entries += far_items([(t, t, q, kind) for t, q, kind in far_own], sums)
        entries.append(("then", far_store({0: 0, 1: 1}, sums, True)))
        for j in range(2):
            side = side_of(j)

            def facing_plane(side=side):
                tile = None
                for d in range(nb):
                    part_copy(e, side, d, left_s).wait_recv()
                    term = part_r[e, side, d]
                    tile = term if tile is None else tile + term
                middle = jnp.where(side == 0, centre_l, centre_r)
                for t, half in enumerate(far_halves(tile)):
                    z = scaled(half, middle, far_rate)
                    z = jnp.where(low_rows, z, 0.0)
                    fST[4 * side + t], fXS[4 * side + t] = source_features(z, part_r[e, side, 0, 4 * t + 3:4 * t + 4, :])

            entries.append(facing_plane)
            sums = {}
            facing = 1 + 3 * side
            entries += far_items([(0, 0, facing, "rim"), (1, 1, facing, "rim"), (2, side, 5 * side, "rim")], sums)
            entries.append(("then", far_store({0: 0, 1: 1, 2: side}, sums, False)))
            if j == 0:
                entries.append(rim_ready(k, 0))
        entries.append(("then", send_far))
        entries += rim_entries(0) + [lambda: springs(k), rim_ready(k, 1)] + rim_entries(1)

        run_stream(entries)

        edge = (e == 0) | (e == EVENTS - 1)
        kick(k, jnp.where(edge, 0.5 * time_step, time_step))
        slow_step = jnp.where(edge, 0.5 * INNER_STEPS * time_step, INNER_STEPS * time_step)
        for copy in part_copies(e) + halo_copies(k) + ring_copies(k):
            copy.wait_send()
        for copy in far_copies(e):
            copy.wait_recv()
        ratio = float(beads_here)
        total = [[None, None] for _ in range(pairs)]
        for d in range(nb):
            tile = far_s[e] if d == 0 else far_r[e, d]
            c = lax.rem(me_b + nb - d, nb)
            turned = pltpu.roll(tile, 4, 0)
            doubled = (jnp.where(low_rows, tile, turned), jnp.where(low_rows, turned, tile))
            for p in range(pairs):
                first = table[c, first_bead + 2 * p] * ratio
                second = table[c, first_bead + 2 * p + 1] * ratio
                level = jnp.where(low_rows, first, second)
                for t in range(2):
                    term = level * doubled[t]
                    total[p][t] = term if d == 0 else total[p][t] + term
        for p in range(pairs):
            for t in range(2):
                lanes = slice(t * PA, (t + 1) * PA)
                V[p, :, lanes] += slow_step * inverse[:, lanes] * total[p][t]

    def outer(e, carry):
        slow_phase(e)

        @pl.when(e < OUTER_STEPS)
        def _():
            drift(INNER_STEPS * e)

            @pl.loop(1, INNER_STEPS)
            def _(i):
                fast_phase(INNER_STEPS * e + i)

        return carry

    lax.fori_loop(0, EVENTS, outer, 0)

    last = PHASES - 1
    for b in range(beads_here):
        p, r = b // 2, 4 * (b % 2)
        for c in range(3):
            result[c, b:b + 1, :] = X[last, p, r + c:r + c + 1, :] - pos[c, b:b + 1, :]
            result[3 + c, b:b + 1, :] = V[p, r + c:r + c + 1, :]

    @pl.loop(0, EVENTS)
    def _(e):
        for copy in far_copies(e):
            copy.wait_send()


def solution(mesh):
    nb, ns = mesh.shape["bead"], mesh.shape["slab"]

    def shards(positions, velocities, masses, amplitudes, charges):
        beads_here, _, atoms = positions.shape
        assert atoms == 2 * PA and beads_here % 2 == 0 and ns > 2
        pairs = beads_here // 2
        table = jnp.asarray(contraction(beads_here * nb, nb))
        vmem = pl.BlockSpec(memory_space=pltpu.VMEM)
        out = jax.ShapeDtypeStruct((3, beads_here, atoms), F32)
        V, D = pltpu.VMEM, pltpu.SemaphoreType.DMA
        tile = (8, PA)

        def body(*refs):
            kernel(nb, ns, 2 * ns, *refs)

        result = pl.pallas_call(
            body,
            name="rod",
            out_shape=pltpu.VMEM((6,) + out.shape[1:], F32),
            in_specs=[pl.BlockSpec(memory_space=pl.ANY)] * 6,
            out_specs=vmem,
            scratch_shapes=[
                pltpu.SMEM(table.shape, F32), V(out.shape, F32), V(out.shape, F32),
                V((1, atoms), F32), V((1, atoms), F32), V((1, atoms), F32), D((6,)),
                V((PHASES, pairs, 8, atoms), F32),
                V((pairs, 8, atoms), F32),
                V((pairs, 8, atoms), F32),
                V((PHASES, 2, pairs) + tile, F32),
                V((PHASES, 8, atoms), F32), V((PHASES, 8, atoms), F32),
                V((EVENTS, nb) + tile, F32), V((EVENTS, 3, nb) + tile, F32),
                V((EVENTS,) + tile, F32),
                V((EVENTS,) + tile, F32), V((EVENTS, nb) + tile, F32),
                V((pairs, 4, PA, FEATURES), BF16), V((pairs, 4, 16, PA), BF16),
                V((pairs, 2, 2, FEATURES, PA), BF16), V((pairs, 2) + tile, F32),
                V((6, PA, FEATURES), BF16), V((6, 16, PA), BF16),
                V((2, FEATURES, PA), BF16), V((2,) + tile, F32),
                D((PHASES, 2)), D((PHASES, 2)), D((PHASES, 2)), D((PHASES, 2)),
                D((EVENTS, 3, nb)), D((EVENTS, 3, nb)),
                D((EVENTS, nb)), D((EVENTS, nb)),
            ],
            compiler_params=pltpu.CompilerParams(collective_id=0, has_side_effects=True),
        )(table, positions.transpose(1, 0, 2), velocities.transpose(1, 0, 2), masses[None], amplitudes[None], charges[None])
        return result[:3].transpose(1, 0, 2), result[3:].transpose(1, 0, 2)

    both = P("bead", None, "slab")
    return jax.shard_map(
        shards, mesh=mesh, in_specs=(both, both, P("slab"), P("slab"), P("slab")), out_specs=(both, both), check_vma=False
    )
```

```python
import math

import jax
import jax.numpy as jnp
import numpy as np
from jax import lax
from jax.experimental import pallas as pl
from jax.experimental.pallas import tpu as pltpu
from jax.sharding import PartitionSpec as P

INNER_STEPS = 2
OUTER_STEPS = 2
PLANE_ATOMS = 512

time_step = 0.05
spring_rate = 25.0
near_scale = 4.0
far_scale = 2.0

MESH = pl.DeviceIdType.MESH
F32 = jnp.float32
BF16 = jnp.bfloat16
PA = PLANE_ATOMS
PHASES = INNER_STEPS * OUTER_STEPS + 1
EVENTS = OUTER_STEPS + 1
FEATURES = 64
HALF = PA // 2


def contraction(bead_count, small_count):
    bead_place = np.arange(bead_count, dtype=np.float64) / bead_count
    small_place = np.arange(small_count, dtype=np.float64) / small_count
    phase = 2.0 * np.pi * (bead_place[None, :] - small_place[:, None])
    modes = np.arange(1, small_count // 2, dtype=np.float64)
    total = 1.0 + np.cos(0.5 * small_count * phase)
    total = total + 2.0 * np.sum(np.cos(modes[:, None, None] * phase[None]), axis=0)
    return (total / bead_count).astype(np.float32)


def rows_of(width):
    return lax.broadcasted_iota(jnp.int32, (8, width), 0)


def cut(x):
    high = x.astype(BF16).astype(F32)
    rest = x - high
    mid = rest.astype(BF16).astype(F32)
    low = (rest - mid).astype(BF16).astype(F32)
    return high, mid, low


def scaled(x, first_centre, rate):
    quarter = rows_of(x.shape[1]) & 3
    centre = jnp.where(quarter == 0, first_centre, jnp.where(quarter == 3, 0.0, 1.0))
    return (x - centre) * rate


def source_features(z, share):
    quarter = rows_of(z.shape[1]) & 3
    square = 0.5 * z * z
    norm = pltpu.roll(square, 1, 0) + pltpu.roll(square, 2, 0) + pltpu.roll(square, 3, 0)
    high, mid, low = cut(jnp.where(quarter == 3, norm, z))
    one = jnp.ones_like(z)
    features = jnp.concatenate([high, high, mid, mid, high, low, one, jnp.zeros_like(z)], axis=0)
    weighted = share * jnp.where(quarter == 3, 1.0, z)
    first, second, _ = cut(weighted)
    return features.T.astype(BF16), jnp.concatenate([first, second], axis=0).astype(BF16)


def target_features(z):
    quarter = rows_of(z.shape[1]) & 3
    square = 0.5 * z * z
    norm = pltpu.roll(square, 1, 0) + pltpu.roll(square, 2, 0) + pltpu.roll(square, 3, 0)
    high, mid, low = cut(jnp.where(quarter == 3, norm, z))
    flat = quarter == 3
    own = jnp.where(
        flat,
        -high,
        jnp.where(quarter == 2, -pltpu.roll(mid, 7, 0), jnp.where(quarter == 1, -pltpu.roll(low, 6, 0), 0.0)),
    )
    high = jnp.where(flat, -1.0, high)
    mid = jnp.where(flat, 0.0, mid)
    low = jnp.where(flat, 0.0, low)
    return [high, mid, high, mid, low, high, own, jnp.zeros_like(z)]


def masked(groups, half):
    keep = (rows_of(groups[0].shape[1]) >> 2) == half
    return jnp.concatenate([jnp.where(keep, g, 0.0) for g in groups], axis=0).astype(BF16)


def weighted_sum(weighted, weight, pieces, flip):
    dims = (((1,), (1 if flip else 0,)), ((), ()))
    high = weight.astype(BF16)
    total = lax.dot_general(weighted, high, dims, preferred_element_type=F32)
    if pieces == 2:
        rest = (weight - high.astype(F32)).astype(BF16)
        total = total + lax.dot_general(weighted, rest, dims, preferred_element_type=F32)
    return total[:8] + total[8:]


def block_items(sources, weighted, targets, t, kind, sums, pieces, others=None):
    items = []
    for h in range(2):
        rows = slice(h * HALF, (h + 1) * HALF)
        width = HALF if kind == "self" and h == 0 else PA
        flips = None
        if kind == "self" and h == 1:
            flips = (weighted, HALF, (t, 1))
        if kind == "cross":
            flips = (others, PA, (1, h))
        items.append((sources, rows, weighted, targets, width, t, flips, sums, pieces))
    return items


def finish(item, exponent):
    _, rows, weighted, _, width, t, flips, sums, pieces = item
    weight = jnp.exp2(exponent)
    direct = weighted_sum(weighted[:, rows], weight, pieces, False)
    for half in range(width // HALF):
        part = direct[:, half * HALF:(half + 1) * HALF]
        sums[t, half] = sums[t, half] + part if (t, half) in sums else part
    if flips is not None:
        shares, depth, key = flips
        part = weighted_sum(shares[:, :depth], weight[:, :depth], pieces, True)
        sums[key] = sums[key] + part if key in sums else part


def run_stream(entries):
    waiting, pending = None, []
    for entry in entries:
        if not isinstance(entry, tuple):
            entry()
            continue
        if entry[0] == "then":
            pending.append(entry[1])
            continue
        if entry[0] == "flush":
            finish(*waiting)
            for act in pending:
                act()
            waiting, pending = None, []
            continue
        sources, rows, _, targets, width = entry[:5]
        exponent = jnp.dot(sources[rows, :], targets[:, :width], preferred_element_type=F32)
        if waiting is not None:
            finish(*waiting)
        for act in pending:
            act()
        waiting, pending = (entry, exponent), []
    finish(*waiting)
    for act in pending:
        act()


def forces_of(z, sums):
    quarter = rows_of(z.shape[1]) & 3
    plain = jnp.where(quarter == 3, sums, 0.0)
    spread = pltpu.roll(plain, 7, 0) + pltpu.roll(plain, 6, 0) + pltpu.roll(plain, 5, 0)
    return jnp.where(quarter == 3, 0.0, z * spread - sums)


def kernel(
    nb, ns, planes_total,
    table_h, pos_h, vel_h, mass_h, amp_h, chg_h,
    result,
    table, pos, vel, mass, amp, chg, in_sem,
    X, V, AF, halo, ring_p, ring_n,
    part_s, part_r, Y, far_s, far_r,
    nST, nXS, nT, nG, fST, fXS, fT, fG,
    halo_ss, halo_rs, ring_ss, ring_rs, part_ss, part_rs, far_ss, far_rs,
):
    me_b = lax.axis_index("bead")
    me_s = lax.axis_index("slab")
    left_s = lax.rem(me_s + ns - 1, ns)
    right_s = lax.rem(me_s + 1, ns)
    left = (me_b, left_s)
    right = (me_b, right_s)
    prev = (lax.rem(me_b + nb - 1, nb), me_s)
    after = (lax.rem(me_b + 1, nb), me_s)
    pairs = X.shape[1]
    beads_here = 2 * pairs
    atoms = X.shape[3]
    first_bead = me_b * beads_here

    def peer(d):
        return lax.rem(me_b + d, nb)

    def remote(src, dst, ss, rs, to):
        return pltpu.make_async_remote_copy(
            src_ref=src, dst_ref=dst, send_sem=ss, recv_sem=rs, device_id=to, device_id_type=MESH
        )

    barrier = pltpu.get_barrier_semaphore()
    for d in range(nb):
        for side in (left_s, right_s):
            pl.semaphore_signal(barrier, inc=1, device_id=(peer(d), side), device_id_type=MESH)
    for d in range(1, nb):
        other = (lax.rem(me_b + d, nb), me_s)
        pl.semaphore_signal(barrier, inc=1, device_id=other, device_id_type=MESH)

    loads = [
        pltpu.make_async_copy(src, dst, in_sem.at[i])
        for i, (src, dst) in enumerate(
            ((pos_h, pos), (vel_h, vel), (amp_h, amp), (chg_h, chg), (mass_h, mass), (table_h, table))
        )
    ]
    for load in loads:
        load.start()
    X[0] = jnp.zeros((pairs, 8, atoms), F32)
    V[...] = jnp.zeros_like(V)
    for load in loads:
        load.wait()
    for b in range(beads_here):
        p, r = b // 2, 4 * (b % 2)
        for c in range(3):
            X[0, p, r + c:r + c + 1, :] = pos[c, b:b + 1, :]
            V[p, r + c:r + c + 1, :] = vel[c, b:b + 1, :]
    for p in range(pairs):
        for r in (3, 7):
            X[0, p, r:r + 1, :] = amp[...]
    quarter = rows_of(PA) & 3
    charges = jnp.where(rows_of(PA) < 4, chg[:, :PA], chg[:, PA:])

    centre = (me_s * 2).astype(F32) + 1.0
    span = float(planes_total)
    centre_l = centre + jnp.where(me_s == 0, span, 0.0)
    centre_r = centre - jnp.where(me_s == ns - 1, span, 0.0)
    near_rate = math.sqrt(near_scale / math.log(2.0))
    far_rate = math.sqrt(far_scale / math.log(2.0))

    inverse = 1.0 / mass[...]

    pl.semaphore_wait(barrier, 3 * nb - 1)

    def halo_copies(k):
        return [
            remote(X.at[k, :, :, pl.ds(0, PA)], halo.at[k, 1], halo_ss.at[k, 1], halo_rs.at[k, 1], left),
            remote(X.at[k, :, :, pl.ds(atoms - PA, PA)], halo.at[k, 0], halo_ss.at[k, 0], halo_rs.at[k, 0], right),
        ]

    def halo_from(k, side):
        return remote(X.at[k, :, :, pl.ds(0, PA)], halo.at[k, side], halo_ss.at[k, side], halo_rs.at[k, side], left)

    def ring_copies(k):
        return [
            remote(X.at[k, pairs - 1], ring_p.at[k], ring_ss.at[k, 0], ring_rs.at[k, 0], after),
            remote(X.at[k, 0], ring_n.at[k], ring_ss.at[k, 1], ring_rs.at[k, 1], prev),
        ]

    def far_copies(e):
        return [
            remote(far_s.at[e], far_r.at[e, d], far_ss.at[e, d], far_rs.at[e, d], (lax.rem(me_b + d, nb), me_s))
            for d in range(1, nb)
        ]

    def part_copy(e, place, d, to):
        return remote(
            part_s.at[e, d], part_r.at[e, place, d], part_ss.at[e, place, d], part_rs.at[e, place, d], (peer(d), to)
        )

    def parts_to(e, d):
        sides = [part_copy(e, 1, d, left_s), part_copy(e, 0, d, right_s)]
        return sides + ([part_copy(e, 2, d, me_s)] if d else [])

    def part_copies(e):
        return [copy for d in range(nb) for copy in parts_to(e, d)]

    low_rows = rows_of(PA) < 4

    def partial_of(k, c):
        total = None
        for p in range(pairs):
            first = table[c, first_bead + 2 * p]
            second = table[c, first_bead + 2 * p + 1]
            term = jnp.where(rows_of(atoms) < 4, first, second) * X[k, p]
            total = term if total is None else total + term
        total = total + pltpu.roll(total, 4, 0)
        return jnp.where(low_rows, total[:, :PA], total[:, PA:])

    def far_halves(tile):
        first = jnp.where(low_rows, tile, 0.0)
        second = jnp.where(low_rows, pltpu.roll(tile, 4, 0), 0.0)
        return first, second

    def side_of(j):
        return jnp.where(lax.rem(me_s, 2) == 0, 1 - j, j)

    near_own = ((0, 1, "self"), (0, 2, "cross"), (1, 2, "self"))
    far_own = ((0, 2, "self"), (0, 3, "cross"), (1, 3, "self"))

    def near_own_items(p, part, sums):
        items = []
        for t, q, kind in near_own:
            others = nXS.at[p, 1] if kind == "cross" else None
            items += block_items(nST.at[p, q], nXS.at[p, q], nT.at[p, t, part], t, kind, sums, 1, others)
        return items

    def far_items(blocks, sums):
        items = []
        for label, t, q, kind in blocks:
            others = fXS.at[2] if kind == "cross" else None
            items += block_items(fST.at[q], fXS.at[q], fT.at[t], label, kind, sums, 2, others)
        return items

    def near_store(p, sums):
        def act():
            for t, half in sums[0]:
                lanes = slice(half * HALF, (half + 1) * HALF)
                nG[p, t, :, lanes] = jnp.where(rows_of(HALF) < 4, sums[0][t, half], sums[1][t, half])
        return act

    def near_add(p, side, sums):
        def act():
            for half in range(2):
                lanes = slice(half * HALF, (half + 1) * HALF)
                nG[p, side, :, lanes] += jnp.where(rows_of(HALF) < 4, sums[0][0, half], sums[1][0, half])
        return act

    def far_store(places, sums, first):
        def act():
            for label, half in sorted(sums):
                lanes = slice(half * HALF, (half + 1) * HALF)
                if first:
                    fG[places[label], :, lanes] = sums[label, half]
                else:
                    fG[places[label], :, lanes] += sums[label, half]
        return act

    def own_features(k):
        for p in range(pairs):
            for t in range(2):
                lanes = slice(t * PA, (t + 1) * PA)
                z = scaled(X[k, p, :, lanes], centre, near_rate)
                nST[p, 1 + t], nXS[p, 1 + t] = source_features(z, amp[:, lanes])
                groups = target_features(z)
                nT[p, t, 0] = masked(groups, 0)
                nT[p, t, 1] = masked(groups, 1)

    def own_entries(after_first=None):
        entries = []
        for p in range(pairs):
            sums = ({}, {})
            for part in range(2):
                entries += near_own_items(p, part, sums[part])
                if p == 0 and part == 0 and after_first is not None:
                    entries.append(after_first)
            entries.append(("then", near_store(p, sums)))
        return entries

    def rim_ready(k, j):
        side = side_of(j)

        def act():
            halo_from(k, side).wait_recv()
            middle = jnp.where(side == 0, centre_l, centre_r)
            share = halo[k, side, 0, 3:4, :]
            for p in range(pairs):
                z = scaled(halo[k, side, p], middle, near_rate)
                nST[p, 3 * side], nXS[p, 3 * side] = source_features(z, share)

        return act

    def rim_entries(j):
        side = side_of(j)
        entries = []
        for p in range(pairs):
            sums = ({}, {})
            for part in range(2):
                entries += block_items(
                    nST.at[p, 3 * side], nXS.at[p, 3 * side], nT.at[p, side, part], 0, "rim", sums[part], 1
                )
            entries.append(("then", near_add(p, side, sums)))
        return entries

    def springs(k):
        for copy in ring_copies(k):
            copy.wait_recv()
        upper = rows_of(atoms) < 4
        rolled = [pltpu.roll(X[k, p], 4, 0) for p in range(pairs)]
        before = [pltpu.roll(ring_p[k], 4, 0)] + rolled
        behind = rolled + [pltpu.roll(ring_n[k], 4, 0)]
        for p in range(pairs):
            bends = 2.0 * X[k, p] - rolled[p] - jnp.where(upper, before[p], behind[p + 1])
            AF[p] = -spring_rate * bends

    def kick(k, fast_step):
        for p in range(pairs):
            for t in range(2):
                lanes = slice(t * PA, (t + 1) * PA)
                z = scaled(X[k, p, :, lanes], centre, near_rate)
                coefficient = amp[:, lanes] * (near_scale / near_rate) * inverse[:, lanes]
                V[p, :, lanes] += fast_step * (AF[p, :, lanes] + coefficient * forces_of(z, nG[p, t]))

    def drift(k):
        for p in range(pairs):
            X[k + 1, p] = X[k, p] + time_step * V[p]

    def fast_phase(k):
        for copy in halo_copies(k) + ring_copies(k):
            copy.start()
        own_features(k)
        entries = own_entries() + [lambda: springs(k), rim_ready(k, 0)] + rim_entries(0)
        run_stream(entries + [rim_ready(k, 1)] + rim_entries(1))
        for copy in halo_copies(k) + ring_copies(k):
            copy.wait_send()
        kick(k, time_step)
        drift(k)

    def slow_phase(e):
        k = INNER_STEPS * e
        for d in range(nb):
            part_s[e, d] = jnp.where(quarter == 3, charges, partial_of(k, peer(d)))
            for copy in parts_to(e, d):
                copy.start()
        own_features(k)

        def send_edges():
            for copy in halo_copies(k) + ring_copies(k):
                copy.start()

        def own_plane():
            total = part_s[e, 0]
            for d in range(1, nb):
                part_copy(e, 2, d, me_s).wait_recv()
                total = total + part_r[e, 2, d]
            Y[e] = total
            for t, half in enumerate(far_halves(total)):
                z = scaled(half, centre, far_rate)
                z = jnp.where(low_rows, z, 0.0)
                fST[2 + t], fXS[2 + t] = source_features(z, chg[:, t * PA:(t + 1) * PA])
                fT[t] = masked(target_features(z), 0)

        def send_far():
            halves = []
            for t, half in enumerate(far_halves(Y[e])):
                lanes = slice(t * PA, (t + 1) * PA)
                z = scaled(half, centre, far_rate)
                coefficient = chg[:, lanes] * (far_scale / far_rate)
                halves.append(coefficient * forces_of(z, fG[t]))
            far_s[e] = jnp.where(low_rows, halves[0], pltpu.roll(halves[1], 4, 0))
            for copy in far_copies(e):
                copy.start()

        sums = {}
        entries = own_entries(send_edges) + [own_plane]
        entries += far_items([(t, t, q, kind) for t, q, kind in far_own], sums)
        entries.append(("then", far_store({0: 0, 1: 1}, sums, True)))
        for j in range(2):
            side = side_of(j)

            def facing_plane(side=side):
                tile = None
                for d in range(nb):
                    part_copy(e, side, d, left_s).wait_recv()
                    term = part_r[e, side, d]
                    tile = term if tile is None else tile + term
                middle = jnp.where(side == 0, centre_l, centre_r)
                for t, half in enumerate(far_halves(tile)):
                    z = scaled(half, middle, far_rate)
                    z = jnp.where(low_rows, z, 0.0)
                    fST[4 * side + t], fXS[4 * side + t] = source_features(z, part_r[e, side, 0, 4 * t + 3:4 * t + 4, :])

            entries.append(facing_plane)
            sums = {}
            facing = 1 + 3 * side
            entries += far_items([(0, 0, facing, "rim"), (1, 1, facing, "rim"), (2, side, 5 * side, "rim")], sums)
            entries.append(("then", far_store({0: 0, 1: 1, 2: side}, sums, False)))
        entries += [("then", send_far), ("flush",), rim_ready(k, 0)]
        entries += rim_entries(0) + [lambda: springs(k), rim_ready(k, 1)] + rim_entries(1)

        run_stream(entries)

        edge = (e == 0) | (e == EVENTS - 1)
        kick(k, jnp.where(edge, 0.5 * time_step, time_step))
        slow_step = jnp.where(edge, 0.5 * INNER_STEPS * time_step, INNER_STEPS * time_step)
        for copy in part_copies(e) + halo_copies(k) + ring_copies(k):
            copy.wait_send()
        for copy in far_copies(e):
            copy.wait_recv()
        ratio = float(beads_here)
        total = [[None, None] for _ in range(pairs)]
        for d in range(nb):
            tile = far_s[e] if d == 0 else far_r[e, d]
            c = lax.rem(me_b + nb - d, nb)
            turned = pltpu.roll(tile, 4, 0)
            doubled = (jnp.where(low_rows, tile, turned), jnp.where(low_rows, turned, tile))
            for p in range(pairs):
                first = table[c, first_bead + 2 * p] * ratio
                second = table[c, first_bead + 2 * p + 1] * ratio
                level = jnp.where(low_rows, first, second)
                for t in range(2):
                    term = level * doubled[t]
                    total[p][t] = term if d == 0 else total[p][t] + term
        for p in range(pairs):
            for t in range(2):
                lanes = slice(t * PA, (t + 1) * PA)
                V[p, :, lanes] += slow_step * inverse[:, lanes] * total[p][t]

    def outer(e, carry):
        slow_phase(e)

        @pl.when(e < OUTER_STEPS)
        def _():
            drift(INNER_STEPS * e)

            @pl.loop(1, INNER_STEPS)
            def _(i):
                fast_phase(INNER_STEPS * e + i)

        return carry

    lax.fori_loop(0, EVENTS, outer, 0)

    last = PHASES - 1
    for b in range(beads_here):
        p, r = b // 2, 4 * (b % 2)
        for c in range(3):
            result[c, b:b + 1, :] = X[last, p, r + c:r + c + 1, :] - pos[c, b:b + 1, :]
            result[3 + c, b:b + 1, :] = V[p, r + c:r + c + 1, :]

    @pl.loop(0, EVENTS)
    def _(e):
        for copy in far_copies(e):
            copy.wait_send()


def solution(mesh):
    nb, ns = mesh.shape["bead"], mesh.shape["slab"]

    def shards(positions, velocities, masses, amplitudes, charges):
        beads_here, _, atoms = positions.shape
        assert atoms == 2 * PA and beads_here % 2 == 0 and ns > 2
        pairs = beads_here // 2
        table = jnp.asarray(contraction(beads_here * nb, nb))
        vmem = pl.BlockSpec(memory_space=pltpu.VMEM)
        out = jax.ShapeDtypeStruct((3, beads_here, atoms), F32)
        V, D = pltpu.VMEM, pltpu.SemaphoreType.DMA
        tile = (8, PA)

        def body(*refs):
            kernel(nb, ns, 2 * ns, *refs)

        result = pl.pallas_call(
            body,
            name="rod",
            out_shape=pltpu.VMEM((6,) + out.shape[1:], F32),
            in_specs=[pl.BlockSpec(memory_space=pl.ANY)] * 6,
            out_specs=vmem,
            scratch_shapes=[
                pltpu.SMEM(table.shape, F32), V(out.shape, F32), V(out.shape, F32),
                V((1, atoms), F32), V((1, atoms), F32), V((1, atoms), F32), D((6,)),
                V((PHASES, pairs, 8, atoms), F32),
                V((pairs, 8, atoms), F32),
                V((pairs, 8, atoms), F32),
                V((PHASES, 2, pairs) + tile, F32),
                V((PHASES, 8, atoms), F32), V((PHASES, 8, atoms), F32),
                V((EVENTS, nb) + tile, F32), V((EVENTS, 3, nb) + tile, F32),
                V((EVENTS,) + tile, F32),
                V((EVENTS,) + tile, F32), V((EVENTS, nb) + tile, F32),
                V((pairs, 4, PA, FEATURES), BF16), V((pairs, 4, 16, PA), BF16),
                V((pairs, 2, 2, FEATURES, PA), BF16), V((pairs, 2) + tile, F32),
                V((6, PA, FEATURES), BF16), V((6, 16, PA), BF16),
                V((2, FEATURES, PA), BF16), V((2,) + tile, F32),
                D((PHASES, 2)), D((PHASES, 2)), D((PHASES, 2)), D((PHASES, 2)),
                D((EVENTS, 3, nb)), D((EVENTS, 3, nb)),
                D((EVENTS, nb)), D((EVENTS, nb)),
            ],
            compiler_params=pltpu.CompilerParams(collective_id=0, has_side_effects=True),
        )(table, positions.transpose(1, 0, 2), velocities.transpose(1, 0, 2), masses[None], amplitudes[None], charges[None])
        return result[:3].transpose(1, 0, 2), result[3:].transpose(1, 0, 2)

    both = P("bead", None, "slab")
    return jax.shard_map(
        shards, mesh=mesh, in_specs=(both, both, P("slab"), P("slab"), P("slab")), out_specs=(both, both), check_vma=False
    )
```
